32 devices in a mesh: slab: 4 (over x, core), kt: 8 (over z, y).
Axes of the slice: x: 2, y: 2, z: 4, core: 2. Of those that a mesh axis runs over, the one named last changes fastest.
Arguments:
- energies: float32 [4], replicated, may hold values from -0.5 to 0.1
- onsite: float32 [8, 4, 384], P('kt', 'slab'), may hold values from -3.5 to -2.5
- hamiltonian: bfloat16 [8, 4, 2, 384, 384], P('kt', 'slab'), may hold values from -0.109375 to 0.109375
- hopping: bfloat16 [8, 4, 2, 384, 384], P('kt', 'slab'), may hold values from -0.15625 to 0.15625
- contact: bfloat16 [8, 2, 384, 384], P('kt'), may hold values from -2 to 2
- previous: bfloat16 [8, 4, 4, 2, 2, 384, 384], P('kt', None, 'slab'), may hold values from -4 to 4
- neighbours: int32 [8, 2], P('kt'), may hold values from 0 to 7, as said below
- mode_index: int32 [8, 2], P('kt'), may hold values from 0 to 3
- mode_strength: float32 [4], replicated, may hold values from 0.25 to 1
Outputs:
- retarded: bfloat16 [8, 4, 4, 2, 384, 384], P('kt', None, 'slab')
- lesser: bfloat16 [8, 4, 4, 2, 384, 384], P('kt', None, 'slab')
The draws below stay inside these ranges and needn't reach their ends.
Inputs may be any that keep to these rules, and one draw needn't show every extreme that they name: neighbours[k, 0] is k - 1 or k - 2 and neighbours[k, 1] is k + 1 or k + 2, modulo 8.
All inputs are finite; a program needn't handle non-finite values.
Results may differ from the reference program's by a relative error of at most 0.017.
Values may be sent and summed in bfloat16 or wider, within the bound.
A program may use at most 128 MiB of HBM per device.

```python
import math
import jax
import jax.numpy as jnp
from jax import lax

B = 384
NE = 4
MODES = 4
NSL = 4
K = 8


def draw_previous(key, part):
    full_shape = (K, NE, NSL, 2, 2, B, B)
    values = jax.random.truncated_normal(key, -4.0, 4.0, full_shape, jnp.float32)
    kinds = jnp.arange(2).reshape(1, 1, 1, 2, 1, 1, 1)
    factor = jnp.where(kinds == 0, 1.0 / math.sqrt(B), 1.0)
    return (values * factor).astype(jnp.bfloat16)


def draw_contact(key, part):
    full_shape = (K, 2, B, B)
    key_off = jax.random.fold_in(key, 11)
    key_real = jax.random.fold_in(key, 12)
    key_imag = jax.random.fold_in(key, 13)
    spread = jax.random.truncated_normal(key_off, -4.0, 4.0, full_shape, jnp.float32)
    level_real = jax.random.uniform(key_real, (K, B), jnp.float32, -0.3, 0.3)
    level_imag = jnp.exp(jax.random.uniform(key_imag, (K, B), jnp.float32, math.log(0.5), math.log(1.5)))
    identity = jnp.eye(B, dtype=jnp.float32)
    diagonal_part = jnp.stack([level_real[:, :, None] * identity[None], -level_imag[:, :, None] * identity[None]], axis=1)
    values = spread * (0.5 / math.sqrt(B)) + diagonal_part
    return values.astype(jnp.bfloat16)


def draw_neighbours(key, part):
    distance = jax.random.randint(key, (K, 2), 1, 3)
    kpoints = jnp.arange(K)
    backward = (kpoints - distance[:, 0]) % K
    forward = (kpoints + distance[:, 1]) % K
    return jnp.stack([backward, forward], axis=1).astype(jnp.int32)


def touch_ends(drawn, rng, smallest, top_value):
    shape = drawn.shape
    place = [jax.random.randint(jax.random.fold_in(rng, axis), (), 0, shape[axis]) for axis in range(len(shape))]
    drawn = drawn.at[tuple(place)].set(smallest)
    longest = shape.index(max(shape))
    place[longest] = (place[longest] + 1) % shape[longest]
    return drawn.at[tuple(place)].set(top_value)


def steps_of(stream_key, shape, split, smallest, largest):
    def one(position, blocks):
        draws = jax.random.uniform(jax.random.fold_in(jax.random.fold_in(stream_key, 6), position), (blocks,), jnp.float32, smallest / len(split), largest / len(split))
        return jnp.repeat(jnp.exp(draws), shape[position] // blocks).reshape((-1,) + (1,) * (len(shape) - position - 1))

    factor_of = one(*split[0])
    for cut in split[1:]:
        factor_of = factor_of * one(*cut)
    return factor_of


def noise(key, extent, width, reach, cuts=(), kind=jnp.bfloat16):
    gain = steps_of(key, extent, cuts, -0.22, 0.18) if cuts else 1.0
    values = jax.random.normal(key, extent, jnp.float32) * width * gain
    return jnp.minimum(jnp.maximum(values, -reach), reach).astype(kind)


def setup_inputs(seed: int = 0) -> dict:
    key_of = jax.random.split(jax.random.key(seed), 10)
    return {
        "energies": jnp.clip(jax.random.uniform(key_of[0], (NE,), jnp.float32, -0.5, 0.1), -0.5, 0.1),
        "onsite": jnp.clip(-3.5 + 1.0 * jax.random.uniform(key_of[1], (K, NSL, B), jnp.float32) ** steps_of(key_of[1], (K, NSL, B), ((0, 8), (1, 4)), -0.2, 0.2), -3.5, -2.5),
        "hamiltonian": noise(key_of[2], (K, NSL, 2, B, B), (8 * B) ** -0.5, 0.109375, ((0, 8), (1, 4))),
        "hopping": noise(key_of[3], (K, NSL, 2, B, B), (4 * B) ** -0.5, 0.15625, ((0, 8), (1, 4))),
        "contact": draw_contact(jax.random.fold_in(key_of[9], 71), 0),
        "previous": draw_previous(jax.random.fold_in(key_of[9], 71), 0),
        "neighbours": draw_neighbours(jax.random.fold_in(key_of[9], 71), 0),
        "mode_index": touch_ends(jax.random.randint(key_of[7], (K, 2), 0, MODES), jax.random.fold_in(key_of[7], 1), 0, MODES - 1).astype(jnp.int32),
        "mode_strength": jnp.clip(jnp.exp(jax.random.uniform(key_of[8], (MODES,), jnp.float32, math.log(0.25), math.log(1.0))), 0.25, 1.0),
    }


broaden = 0.05
fermi_level = 0.0
thermal = 0.1


def complex_mul(first_op, second_op):
    real_real = jnp.dot(first_op[0], second_op[0], preferred_element_type=jnp.float32)
    imag_imag = jnp.dot(first_op[1], second_op[1], preferred_element_type=jnp.float32)
    real_imag = jnp.dot(first_op[0], second_op[1], preferred_element_type=jnp.float32)
    imag_real = jnp.dot(first_op[1], second_op[0], preferred_element_type=jnp.float32)
    return jnp.stack([real_real - imag_imag, real_imag + imag_real])


def adjoint(matrix):
    return jnp.stack([matrix[0].T, -matrix[1].T])


def slab_update(boundary, energy, levels, hamilton, coupling, phonon):
    conjugate = adjoint(coupling)
    moved_r = complex_mul(coupling, boundary[0]).astype(jnp.bfloat16)
    moved_l = complex_mul(coupling, boundary[1]).astype(jnp.bfloat16)
    self_retarded = complex_mul(moved_r, conjugate)
    self_lesser = complex_mul(moved_l, conjugate)
    identity = jnp.eye(levels.shape[0], dtype=jnp.float32)
    system_real = (energy - levels)[:, None] * identity - hamilton[0].astype(jnp.float32) - self_retarded[0] - phonon[0, 0]
    system_imaginary = broaden * identity - hamilton[1].astype(jnp.float32) - self_retarded[1] - phonon[0, 1]
    diagonal_real = jnp.diagonal(system_real)
    diagonal_imaginary = jnp.diagonal(system_imaginary)
    modulus = diagonal_real * diagonal_real + diagonal_imaginary * diagonal_imaginary
    inverse_real = diagonal_real / modulus
    inverse_imaginary = -diagonal_imaginary / modulus
    scaled_real = inverse_real[:, None] * system_real - inverse_imaginary[:, None] * system_imaginary
    scaled_imaginary = inverse_real[:, None] * system_imaginary + inverse_imaginary[:, None] * system_real
    sandwich_real = scaled_real * inverse_real[None, :] - scaled_imaginary * inverse_imaginary[None, :]
    sandwich_imaginary = scaled_real * inverse_imaginary[None, :] + scaled_imaginary * inverse_real[None, :]
    first_guess = jnp.stack([2.0 * jnp.diag(inverse_real) - sandwich_real, 2.0 * jnp.diag(inverse_imaginary) - sandwich_imaginary])
    first_rounded = first_guess.astype(jnp.bfloat16)
    system_rounded = jnp.stack([system_real, system_imaginary]).astype(jnp.bfloat16)
    product = complex_mul(system_rounded, first_rounded).astype(jnp.bfloat16)
    retarded = (2.0 * first_guess - complex_mul(first_rounded, product)).astype(jnp.bfloat16)
    source = (phonon[1] + self_lesser).astype(jnp.bfloat16)
    halfway = complex_mul(retarded, source).astype(jnp.bfloat16)
    lesser = complex_mul(halfway, adjoint(retarded)).astype(jnp.bfloat16)
    return retarded, lesser


def reference(energies, onsite, hamiltonian, hopping, contact, previous, neighbours, mode_index, mode_strength):
    points = neighbours.shape[0]
    slab_count = onsite.shape[1]

    def one_point(kpoint):
        neighbour_pair = neighbours[kpoint]
        chosen = mode_index[kpoint]
        strength = mode_strength[chosen]
        phonon = strength[0] * previous[neighbour_pair[0]].astype(jnp.float32) + strength[1] * previous[neighbour_pair[1]].astype(jnp.float32)
        contact_block = contact[kpoint]
        contact_float = contact_block.astype(jnp.float32)
        skew_part = jnp.stack([contact_float[0] - contact_float[0].T, contact_float[1] + contact_float[1].T])

        def one_energy(energy, phonon_energy):
            occupation = 1.0 / (1.0 + jnp.exp((energy - fermi_level) / thermal))
            boundary = jnp.stack([contact_block, (-occupation * skew_part).astype(jnp.bfloat16)])
            retarded_list = [None] * slab_count
            lesser_list = [None] * slab_count
            for slab_num in reversed(range(slab_count)):
                ret_block, les_block = slab_update(boundary, energy, onsite[kpoint, slab_num], hamiltonian[kpoint, slab_num], hopping[kpoint, slab_num], phonon_energy[slab_num])
                retarded_list[slab_num] = ret_block
                lesser_list[slab_num] = les_block
                boundary = jnp.stack([ret_block, les_block])
            return jnp.stack(retarded_list), jnp.stack(lesser_list)

        return jax.vmap(one_energy)(energies, phonon)

    retarded, lesser = lax.map(one_point, jnp.arange(points, dtype=jnp.int32))
    return retarded, lesser
```

```python
import functools

import jax
import jax.numpy as jnp
from jax import lax
from jax.experimental import pallas as pl
from jax.experimental.pallas import tpu as pltpu
from jax.sharding import PartitionSpec as P

broaden = 0.05
fermi_level = 0.0
thermal = 0.1

MESH = pl.DeviceIdType.MESH
LEAD = 2
F32 = jnp.float32
BF16 = jnp.bfloat16


def dot(a, b):
    return jnp.dot(a, b, preferred_element_type=F32)


def dot_nt(a, b):
    return lax.dot_general(a, b, (((1,), (1,)), ((), ())), preferred_element_type=F32)


def kernel(
    slabs, points, ne, b,
    scal, flag_in, onsite, ham, hop, contact, prev,
    ret_out, les_out,
    own, mate, zsel, zraw, flag, bx, bl, chat, rhat, les, wide, fhat, mv, sysb, acc, first,
    own_sem, y_send, y_recv, s_send, s_recv, r_send, r_recv, f_sem, b_send, b_recv, o_sem,
):
    slab = lax.axis_index("slab")
    k = lax.axis_index("kt")
    pieces = 2 * ne
    step = 2 - 4 * lax.rem(k, 2)
    mate_k = k + 1 - 2 * lax.rem(k, 2)
    sel_k = lax.rem(k + step + points, points)
    raw_k = lax.rem(k - step + points, points)
    last = slabs - 1
    bands = [(n, min(256, 2 * b - n)) for n in range(0, 2 * b, 256)]
    rows_per = 48

    barrier = pltpu.get_barrier_semaphore()
    for other in (mate_k, sel_k, raw_k):
        pl.semaphore_signal(barrier, inc=1, device_id={"kt": other}, device_id_type=MESH)
    for by in (1, slabs - 1):
        pl.semaphore_signal(
            barrier, inc=1, device_id={"slab": lax.rem(slab + by, slabs)}, device_id_type=MESH
        )
    pl.semaphore_wait(barrier, 5)

    def source(p):
        return prev.at[lax.rem(p, ne), p // ne]

    def y_copy(p):
        return pltpu.make_async_remote_copy(
            source(p), mate.at[p], y_send.at[p], y_recv.at[p],
            device_id={"kt": mate_k}, device_id_type=MESH,
        )

    def raw_copy(p):
        return pltpu.make_async_remote_copy(
            source(p), zraw.at[p], r_send.at[p], r_recv.at[p],
            device_id={"kt": raw_k}, device_id_type=MESH,
        )

    def sel_copy(p):
        return pltpu.make_async_remote_copy(
            own.at[p], zsel.at[p], s_send.at[p], s_recv.at[p],
            device_id={"kt": sel_k}, device_id_type=MESH,
        )

    def own_copy(p):
        return pltpu.make_async_copy(source(p), own.at[p], own_sem.at[p])

    flag_copy = pltpu.make_async_remote_copy(
        flag_in, flag, f_sem.at[0], f_sem.at[1], device_id={"kt": raw_k}, device_id_type=MESH
    )

    def ret_copy(e):
        return pltpu.make_async_remote_copy(
            rhat.at[e, pl.ds(0, b)], bx.at[e], b_send.at[e], b_recv.at[e],
            device_id={"slab": jnp.maximum(slab - 1, 0)}, device_id_type=MESH,
        )

    def les_copy(e):
        return pltpu.make_async_remote_copy(
            les.at[e], bl.at[e], b_send.at[ne + e], b_recv.at[ne + e],
            device_id={"slab": jnp.maximum(slab - 1, 0)}, device_id_type=MESH,
        )

    def ret_store(e, part):
        return pltpu.make_async_copy(
            rhat.at[e, pl.ds(0, b), pl.ds(part * b, b)], ret_out.at[e, part], o_sem.at[e, part]
        )

    def les_store(e, part):
        return pltpu.make_async_copy(
            les.at[e, :, pl.ds(part * b, b)], les_out.at[e, part], o_sem.at[ne + e, part]
        )

    flag_copy.start()
    for p in range(LEAD):
        y_copy(p).start()
        raw_copy(p).start()
        own_copy(p).start()

    def expand(ref):
        ref[b:, 0:b] = -ref[0:b, b:]
        ref[b:, b:] = ref[0:b, 0:b]

    chat[0:b, 0:b] = hop[0]
    chat[0:b, b:] = hop[1]
    expand(chat)

    @pl.when(slab == last)
    def _():
        for part in range(2):
            value = contact[part].astype(F32)
            flipped = value.T
            skew = value - flipped if part == 0 else value + flipped
            acc[:, part * b : (part + 1) * b] = skew
            for e in range(ne):
                bx[e, :, part * b : (part + 1) * b] = contact[part]
        for e in range(ne):
            bl[e] = (-scal[ne + e] * acc[...]).astype(BF16)

    flag_copy.wait()
    weight_sel = scal[2 * ne]
    weight_mate = scal[2 * ne + 1]
    weight_raw = scal[2 * ne + 2]

    def phonon(p, part, rows):
        return (
            weight_sel * zsel[p, part, rows].astype(F32)
            + weight_mate * mate[p, part, rows].astype(F32)
            + weight_raw * zraw[p, part, rows].astype(F32)
        )

    def over_rows(do):
        def one(i, carry):
            do(pl.ds(pl.multiple_of(i * rows_per, rows_per), rows_per))
            return carry

        lax.fori_loop(0, b // rows_per, one, 0)

    def prep(p):
        y_copy(p).wait_recv()
        own_copy(p).wait()

        def pick(rows):
            chosen = flag[0:1, :]
            for part in range(2):
                own[p, part, rows] = (
                    chosen * mate[p, part, rows].astype(F32)
                    + (1.0 - chosen) * own[p, part, rows].astype(F32)
                ).astype(BF16)

        over_rows(pick)
        sel_copy(p).start()

        @pl.when(p + LEAD < pieces)
        def _():
            y_copy(p + LEAD).start()
            raw_copy(p + LEAD).start()
            own_copy(p + LEAD).start()

    def self_energy(boundary):
        wide[0:b, :] = boundary[...]
        expand(wide)
        for n, w in bands:
            mv[:, n : n + w] = dot(chat[0:b, :], wide[:, n : n + w]).astype(BF16)
        for n, w in bands:
            acc[:, n : n + w] = dot_nt(mv[...], chat[n : n + w, :])

    def ret_stage(e):
        @pl.when(slab < last)
        def _():
            ret_copy(e).wait_recv()

        self_energy(bx.at[e])
        sel_copy(e).wait_recv()
        raw_copy(e).wait_recv()
        energy = scal[e]

        def make_system(rows):
            at = lax.broadcasted_iota(jnp.int32, (rows_per, b), 0) + rows.start
            eye = at == lax.broadcasted_iota(jnp.int32, (rows_per, b), 1)
            real = jnp.where(eye, energy - onsite[...], 0.0)
            imag = jnp.where(eye, broaden, 0.0)
            for part, diagonal in ((0, real), (1, imag)):
                columns = slice(part * b, (part + 1) * b)
                value = (
                    diagonal - ham[part, rows].astype(F32) - acc[rows, columns] - phonon(e, part, rows)
                )
                acc[rows, columns] = value
                sysb[rows, columns] = value.astype(BF16)

        over_rows(make_system)
        eye = lax.broadcasted_iota(jnp.int32, (128, 128), 0) == lax.broadcasted_iota(
            jnp.int32, (128, 128), 1
        )
        across, along = [], []
        for i in range(b // 128):
            rows = slice(i * 128, (i + 1) * 128)
            real = jnp.where(eye, acc[rows, i * 128 : (i + 1) * 128], 0.0)
            imag = jnp.where(eye, acc[rows, b + i * 128 : b + (i + 1) * 128], 0.0)
            for axis, found in ((0, across), (1, along)):
                re = jnp.sum(real, axis=axis, keepdims=True)
                im = jnp.sum(imag, axis=axis, keepdims=True)
                modulus = re * re + im * im
                found.append((re / modulus, -im / modulus))
        row_re = jnp.concatenate([found[0] for found in across], axis=1)
        row_im = jnp.concatenate([found[1] for found in across], axis=1)
        for i in range(b // 128):
            col_re, col_im = along[i]
            for half in range(2):
                start = i * 128 + half * 64
                rows = slice(start, start + 64)
                cre = col_re[half * 64 : half * 64 + 64]
                cim = col_im[half * 64 : half * 64 + 64]
                re, im = acc[rows, 0:b], acc[rows, b:]
                scaled_re = cre * re - cim * im
                scaled_im = cre * im + cim * re
                on = (
                    lax.broadcasted_iota(jnp.int32, (64, b), 0) + start
                    == lax.broadcasted_iota(jnp.int32, (64, b), 1)
                )
                first_re = jnp.where(on, 2.0 * row_re, 0.0) - (scaled_re * row_re - scaled_im * row_im)
                first_im = jnp.where(on, 2.0 * row_im, 0.0) - (scaled_re * row_im + scaled_im * row_re)
                first[rows, 0:b] = first_re
                first[rows, b:] = first_im
                fhat[rows, 0:b] = first_re.astype(BF16)
                fhat[rows, b:] = first_im.astype(BF16)
        expand(fhat)
        for n, w in bands:
            wide[0:b, n : n + w] = dot(sysb[...], fhat[:, n : n + w]).astype(BF16)
        expand(wide)
        for n, w in bands:
            rhat[e, 0:b, n : n + w] = (
                2.0 * first[:, n : n + w] - dot(fhat[0:b, :], wide[:, n : n + w])
            ).astype(BF16)

        @pl.when(slab > 0)
        def _():
            ret_copy(e).start()

        ret_store(e, 0).start()
        ret_store(e, 1).start()
        expand(rhat.at[e])

    def les_stage(e):
        p = ne + e

        @pl.when(slab < last)
        def _():
            les_copy(e).wait_recv()

        self_energy(bl.at[e])
        sel_copy(p).wait_recv()
        raw_copy(p).wait_recv()

        def make_source(rows):
            for part in range(2):
                columns = slice(part * b, (part + 1) * b)
                wide[rows, columns] = (phonon(p, part, rows) + acc[rows, columns]).astype(BF16)

        over_rows(make_source)
        expand(wide)
        for n, w in bands:
            mv[:, n : n + w] = dot(rhat[e, 0:b, :], wide[:, n : n + w]).astype(BF16)
        for n, w in bands:
            les[e, :, n : n + w] = dot_nt(mv[...], rhat[e, n : n + w, :]).astype(BF16)

        @pl.when(slab > 0)
        def _():
            les_copy(e).start()

        les_store(e, 0).start()
        les_store(e, 1).start()

    def turn(t, carry):
        @pl.when(t < pieces)
        def _():
            prep(t)

        c = t - LEAD

        @pl.when(jnp.logical_and(c >= 0, c < ne))
        def _():
            ret_stage(c)

        @pl.when(c >= ne)
        def _():
            les_stage(c - ne)

        return carry

    lax.fori_loop(0, pieces + LEAD, turn, 0)

    def drain(p, carry):
        y_copy(p).wait_send()
        raw_copy(p).wait_send()
        sel_copy(p).wait_send()
        return carry

    lax.fori_loop(0, pieces, drain, 0)

    def drain_out(e, carry):
        @pl.when(slab > 0)
        def _():
            ret_copy(e).wait_send()
            les_copy(e).wait_send()

        for part in range(2):
            ret_store(e, part).wait()
            les_store(e, part).wait()
        return carry

    lax.fori_loop(0, ne, drain_out, 0)


def body(
    energies, onsite, hamiltonian, hopping, contact, previous, neighbours, mode_index, mode_strength
):
    slabs, points = lax.axis_size("slab"), lax.axis_size("kt")
    k = lax.axis_index("kt")
    ne, b = energies.shape[0], onsite.shape[-1]
    even = k % 2 == 0
    pair = neighbours[0]
    left_near = pair[0] == (k - 1) % points
    right_near = pair[1] == (k + 1) % points
    table = jnp.arange(mode_strength.shape[0], dtype=jnp.int32)
    strength = jnp.sum(
        jnp.where(mode_index[0][:, None] == table[None, :], mode_strength[None, :], 0.0), axis=1
    )
    sel_near = jnp.where(even, left_near, right_near).astype(F32)
    raw_near = jnp.where(even, right_near, left_near).astype(F32)
    weight_sel = jnp.where(even, strength[0], strength[1])
    weight_other = jnp.where(even, strength[1], strength[0])
    occupation = 1.0 / (1.0 + jnp.exp((energies - fermi_level) / thermal))
    scal = jnp.concatenate(
        [
            energies,
            occupation,
            jnp.stack([weight_sel, weight_other * raw_near, weight_other * (1.0 - raw_near)]),
        ]
    )
    flag = jnp.broadcast_to(sel_near, (8, b))
    pieces = 2 * ne
    block = (pieces, 2, b, b)
    cat, square = (b, 2 * b), (2 * b, 2 * b)
    vmem = pl.BlockSpec(memory_space=pltpu.VMEM)
    anywhere = pl.BlockSpec(memory_space=pl.ANY)
    out = jax.ShapeDtypeStruct((ne, 2, b, b), BF16)
    dma = pltpu.SemaphoreType.DMA
    retarded, lesser = pl.pallas_call(
        functools.partial(kernel, slabs, points, ne, b),
        out_shape=(out, out),
        in_specs=[pl.BlockSpec(memory_space=pltpu.SMEM)] + [vmem] * 5 + [anywhere],
        out_specs=(anywhere, anywhere),
        scratch_shapes=[
            pltpu.VMEM(block, BF16),
            pltpu.VMEM(block, BF16),
            pltpu.VMEM(block, BF16),
            pltpu.VMEM(block, BF16),
            pltpu.VMEM((8, b), F32),
            pltpu.VMEM((ne,) + cat, BF16),
            pltpu.VMEM((ne,) + cat, BF16),
            pltpu.VMEM(square, BF16),
            pltpu.VMEM((ne,) + square, BF16),
            pltpu.VMEM((ne,) + cat, BF16),
            pltpu.VMEM(square, BF16),
            pltpu.VMEM(square, BF16),
            pltpu.VMEM(cat, BF16),
            pltpu.VMEM(cat, BF16),
            pltpu.VMEM(cat, F32),
            pltpu.VMEM(cat, F32),
            dma((pieces,)),
            dma((pieces,)),
            dma((pieces,)),
            dma((pieces,)),
            dma((pieces,)),
            dma((pieces,)),
            dma((pieces,)),
            dma((2,)),
            dma((pieces,)),
            dma((pieces,)),
            dma((pieces, 2)),
        ],
        compiler_params=pltpu.CompilerParams(
            collective_id=0, has_side_effects=True, vmem_limit_bytes=56 * 1024 * 1024
        ),
        name="sweep",
    )(
        scal, flag, onsite[0], hamiltonian[0, 0], hopping[0, 0], contact[0],
        previous.reshape((ne, 2, 2, b, b)),
    )
    whole = (1, ne, 1, 2, b, b)
    return retarded.reshape(whole), lesser.reshape(whole)


def solution(mesh):
    in_specs = (
        P(),
        P("kt", "slab", None),
        P("kt", "slab", None, None, None),
        P("kt", "slab", None, None, None),
        P("kt", None, None, None),
        P("kt", None, "slab", None, None, None, None),
        P("kt", None),
        P("kt", None),
        P(),
    )
    out_specs = (P("kt", None, "slab", None, None, None), P("kt", None, "slab", None, None, None))
    return jax.shard_map(body, mesh=mesh, in_specs=in_specs, out_specs=out_specs, check_vma=False)
```

```python
import functools

import jax
import jax.numpy as jnp
from jax import lax
from jax.experimental import pallas as pl
from jax.experimental.pallas import tpu as pltpu
from jax.sharding import PartitionSpec as P

broaden = 0.05
fermi_level = 0.0
thermal = 0.1

MESH = pl.DeviceIdType.MESH
LEAD = 3
AHEAD = 2
F32 = jnp.float32
BF16 = jnp.bfloat16


def dot(a, b):
    return jnp.dot(a, b, preferred_element_type=F32)


def dot_nt(a, b):
    return lax.dot_general(a, b, (((1,), (1,)), ((), ())), preferred_element_type=F32)


def agree(
    points, b,
    energies, neighbours, mode_index, mode_strength,
    table, both_far,
    mine, every, send, recv,
):
    k = lax.axis_index("kt")
    even = lax.rem(k, 2) == 0
    barrier = pltpu.get_barrier_semaphore()

    def peer(by):
        return {"kt": lax.rem(k + by, points)}

    def greet(by, carry):
        pl.semaphore_signal(barrier, inc=1, device_id=peer(by), device_id_type=MESH)
        return carry

    lax.fori_loop(1, points, greet, 0)
    pl.semaphore_wait(barrier, points - 1)
    left = jnp.where(neighbours[0, 0] == lax.rem(k - 1 + points, points), 1.0, 0.0)
    right = jnp.where(neighbours[0, 1] == lax.rem(k + 1, points), 1.0, 0.0)
    row = lax.broadcasted_iota(jnp.int32, (8, 128), 0)
    mine[...] = jnp.where(row == 0, left, right)
    every[k] = mine[...]

    def tell(by):
        return pltpu.make_async_remote_copy(
            mine, every.at[k], send.at[by], recv.at[k], device_id=peer(by), device_id_type=MESH
        )

    def hear(by):
        j = lax.rem(k + by, points)
        return pltpu.make_async_remote_copy(
            mine, every.at[j], send.at[by], recv.at[j], device_id=peer(by), device_id_type=MESH
        )

    def start(by, carry):
        tell(by).start()
        return carry

    def finish(by, carry):
        tell(by).wait_send()
        hear(by).wait_recv()
        return carry

    lax.fori_loop(1, points, start, 0)
    lax.fori_loop(1, points, finish, 0)

    def near(j):
        j = lax.rem(j + points, points)
        return every[j, 0:1, :], every[j, 1:2, :]

    left_2, right_2 = near(k + 2), near(k - 2)
    left_1, right_1 = near(k + 1), near(k - 1)
    chosen = jnp.where(even, left_2[0], right_2[1])
    wrapped = jnp.where(even, right_1[1], left_1[0])
    strength_left = mode_strength[mode_index[0, 0]]
    strength_right = mode_strength[mode_index[0, 1]]
    weight_sel = jnp.where(even, strength_left, strength_right)
    weight_other = jnp.where(even, strength_right, strength_left)
    other_near = jnp.where(even, right, left)
    full = jnp.zeros((1, 128), F32)
    rows = [
        chosen,
        wrapped,
        full + weight_sel,
        full + weight_other * other_near,
        full + weight_other * (1.0 - other_near),
    ]
    for e in range(energies.shape[0]):
        rows.append(1.0 / (1.0 + jnp.exp((full + energies[e] - fermi_level) / thermal)))
    for i, value in enumerate(rows):
        for start_at in range(0, b, 128):
            table[i : i + 1, start_at : start_at + 128] = value
    up = (1.0 - near(0)[0]) * (1.0 - near(1)[0])
    down = (1.0 - near(points - 1)[1]) * (1.0 - near(points - 2)[1])
    both_far[0, 0] = jnp.max(jnp.maximum(up, down))


def kernel(
    halve, slabs, points, ne, b,
    energies, table, onsite, ham, hop, contact, prev,
    ret_out, les_out,
    own, mate, zsel, zraw, stage, bx, bl, chat, rhat, ghat, les, wide, fhat, mv, sysb, acc, first,
    own_sem, y_send, y_recv, s_send, s_recv, r_send, r_recv, f_send, f_recv, b_send, b_recv, o_sem,
):
    slab = lax.axis_index("slab")
    k = lax.axis_index("kt")
    pieces = 2 * ne
    step = 2 - 4 * lax.rem(k, 2)
    parity = lax.rem(k, 2)
    mate_k = k + 1 - 2 * lax.rem(k, 2)
    sel_k = lax.rem(k + step + points, points)
    raw_k = lax.rem(k - step + points, points)
    raw_seam = jnp.logical_and(halve, jnp.logical_or(k == 0, k == points - 1))
    sel_seam = jnp.logical_and(halve, jnp.logical_or(k == 1, k == points - 2))
    last = slabs - 1
    bands = [(n, min(256, 2 * b - n)) for n in range(0, 2 * b, 256)]
    rows_per = 48

    barrier = pltpu.get_barrier_semaphore()
    for other in (mate_k, sel_k, raw_k):
        pl.semaphore_signal(barrier, inc=1, device_id={"kt": other}, device_id_type=MESH)
    for by in (1, slabs - 1):
        pl.semaphore_signal(
            barrier, inc=1, device_id={"slab": lax.rem(slab + by, slabs)}, device_id_type=MESH
        )
    pl.semaphore_wait(barrier, 5)

    def source(p):
        return prev.at[lax.rem(p, ne), p // ne]

    def y_copy(p):
        return pltpu.make_async_remote_copy(
            source(p), mate.at[p], y_send.at[p], y_recv.at[p],
            device_id={"kt": mate_k}, device_id_type=MESH,
        )

    def raw_copy(p):
        return pltpu.make_async_remote_copy(
            source(p), zraw.at[p], r_send.at[p], r_recv.at[p],
            device_id={"kt": raw_k}, device_id_type=MESH,
        )

    def sel_copy(p):
        return pltpu.make_async_remote_copy(
            own.at[p], zsel.at[p], s_send.at[p], s_recv.at[p],
            device_id={"kt": sel_k}, device_id_type=MESH,
        )

    def own_copy(p):
        return pltpu.make_async_copy(source(p), own.at[p], own_sem.at[p])

    def raw_half(p):
        return pltpu.make_async_remote_copy(
            stage.at[p], zraw.at[p, parity], r_send.at[p], r_recv.at[p],
            device_id={"kt": raw_k}, device_id_type=MESH,
        )

    def sel_half(p):
        return pltpu.make_async_remote_copy(
            own.at[p, parity], zsel.at[p, parity], s_send.at[p], s_recv.at[p],
            device_id={"kt": sel_k}, device_id_type=MESH,
        )

    def pass_sel(p, part):
        return pltpu.make_async_remote_copy(
            zsel.at[p, part], zraw.at[p, part], f_send.at[p], f_recv.at[p],
            device_id={"kt": mate_k}, device_id_type=MESH,
        )

    def pass_raw(p, part):
        return pltpu.make_async_remote_copy(
            zraw.at[p, part], zsel.at[p, part], f_send.at[p], f_recv.at[p],
            device_id={"kt": mate_k}, device_id_type=MESH,
        )

    def either(seam, half, whole):
        if not halve:
            whole()
            return
        pl.when(seam)(half)
        pl.when(jnp.logical_not(seam))(whole)

    def nothing():
        return None

    def pass_on(p):
        if not halve:
            return

        @pl.when(raw_seam)
        def _():
            sel_half(p).wait_recv()
            pass_sel(p, parity).start()

        @pl.when(sel_seam)
        def _():
            raw_half(p).wait_recv()
            pass_raw(p, parity).start()

    def arrived(p):
        either(raw_seam, lambda: pass_raw(p, 1 - parity).wait_recv(), lambda: sel_copy(p).wait_recv())
        either(sel_seam, lambda: pass_sel(p, 1 - parity).wait_recv(), lambda: raw_copy(p).wait_recv())

    def ret_copy(e):
        return pltpu.make_async_remote_copy(
            rhat.at[e, pl.ds(0, b)], bx.at[e], b_send.at[e], b_recv.at[e],
            device_id={"slab": jnp.maximum(slab - 1, 0)}, device_id_type=MESH,
        )

    def les_copy(e):
        return pltpu.make_async_remote_copy(
            les.at[e], bl.at[e], b_send.at[ne + e], b_recv.at[ne + e],
            device_id={"slab": jnp.maximum(slab - 1, 0)}, device_id_type=MESH,
        )

    def ret_store(e, part):
        return pltpu.make_async_copy(
            rhat.at[e, pl.ds(0, b), pl.ds(part * b, b)], ret_out.at[e, part], o_sem.at[e, part]
        )

    def les_store(e, part):
        return pltpu.make_async_copy(
            les.at[e, :, pl.ds(part * b, b)], les_out.at[e, part], o_sem.at[ne + e, part]
        )

    def begin(p):
        y_copy(p).start()
        either(raw_seam, nothing, lambda: raw_copy(p).start())
        own_copy(p).start()

    for p in range(AHEAD):
        begin(p)

    def expand(ref):
        ref[b:, 0:b] = -ref[0:b, b:]
        ref[b:, b:] = ref[0:b, 0:b]

    chat[0:b, 0:b] = hop[0]
    chat[0:b, b:] = hop[1]
    expand(chat)

    @pl.when(slab == last)
    def _():
        for part in range(2):
            value = contact[part].astype(F32)
            flipped = value.T
            skew = value - flipped if part == 0 else value + flipped
            acc[:, part * b : (part + 1) * b] = skew
            for e in range(ne):
                bx[e, :, part * b : (part + 1) * b] = contact[part]
        for e in range(ne):
            for part in range(2):
                columns = slice(part * b, (part + 1) * b)
                bl[e, :, columns] = (-table[5 + e : 6 + e, :] * acc[:, columns]).astype(BF16)

    def phonon(p, part, rows):
        return (
            table[2:3, :] * zsel[p, part, rows].astype(F32)
            + table[3:4, :] * mate[p, part, rows].astype(F32)
            + table[4:5, :] * zraw[p, part, rows].astype(F32)
        )

    def over_rows(do):
        def one(i, carry):
            do(pl.ds(pl.multiple_of(i * rows_per, rows_per), rows_per))
            return carry

        lax.fori_loop(0, b // rows_per, one, 0)

    def prep(p):
        y_copy(p).wait_recv()
        own_copy(p).wait()

        def pick_seam(rows):
            chosen = table[1:2, :]
            stage[p, rows] = (
                chosen * own[p, parity, rows].astype(F32)
                + (1.0 - chosen) * mate[p, parity, rows].astype(F32)
            ).astype(BF16)

        def start_seam():
            over_rows(pick_seam)
            raw_half(p).start()

        either(raw_seam, start_seam, nothing)

        def pick(rows):
            chosen = table[0:1, :]
            for part in range(2):
                own[p, part, rows] = (
                    chosen * mate[p, part, rows].astype(F32)
                    + (1.0 - chosen) * own[p, part, rows].astype(F32)
                ).astype(BF16)

        over_rows(pick)
        either(sel_seam, lambda: sel_half(p).start(), lambda: sel_copy(p).start())

        @pl.when(p + AHEAD < pieces)
        def _():
            begin(p + AHEAD)

    def congruence(left, boundary):
        wide[0:b, :] = boundary[...]
        expand(wide)
        for n, w in bands:
            mv[:, n : n + w] = dot(left[0:b, :], wide[:, n : n + w]).astype(BF16)
        return [(n, w, dot_nt(mv[...], left[n : n + w, :])) for n, w in bands]

    def ret_stage(e):
        pass_on(e)

        @pl.when(slab < last)
        def _():
            ret_copy(e).wait_recv()

        for n, w, value in congruence(chat, bx.at[e]):
            acc[:, n : n + w] = value
        arrived(e)
        energy = energies[e]

        def make_system(rows):
            at = lax.broadcasted_iota(jnp.int32, (rows_per, b), 0) + rows.start
            eye = at == lax.broadcasted_iota(jnp.int32, (rows_per, b), 1)
            real = jnp.where(eye, energy - onsite[...], 0.0)
            imag = jnp.where(eye, broaden, 0.0)
            for part, diagonal in ((0, real), (1, imag)):
                columns = slice(part * b, (part + 1) * b)
                value = (
                    diagonal - ham[part, rows].astype(F32) - acc[rows, columns] - phonon(e, part, rows)
                )
                acc[rows, columns] = value
                sysb[rows, columns] = value.astype(BF16)

        over_rows(make_system)
        eye = lax.broadcasted_iota(jnp.int32, (128, 128), 0) == lax.broadcasted_iota(
            jnp.int32, (128, 128), 1
        )
        across, along = [], []
        for i in range(b // 128):
            rows = slice(i * 128, (i + 1) * 128)
            real = jnp.where(eye, acc[rows, i * 128 : (i + 1) * 128], 0.0)
            imag = jnp.where(eye, acc[rows, b + i * 128 : b + (i + 1) * 128], 0.0)
            for axis, found in ((0, across), (1, along)):
                re = jnp.sum(real, axis=axis, keepdims=True)
                im = jnp.sum(imag, axis=axis, keepdims=True)
                modulus = re * re + im * im
                found.append((re / modulus, -im / modulus))
        row_re = jnp.concatenate([found[0] for found in across], axis=1)
        row_im = jnp.concatenate([found[1] for found in across], axis=1)
        for i in range(b // 128):
            col_re, col_im = along[i]
            for half in range(2):
                start = i * 128 + half * 64
                rows = slice(start, start + 64)
                cre = col_re[half * 64 : half * 64 + 64]
                cim = col_im[half * 64 : half * 64 + 64]
                re, im = acc[rows, 0:b], acc[rows, b:]
                scaled_re = cre * re - cim * im
                scaled_im = cre * im + cim * re
                on = (
                    lax.broadcasted_iota(jnp.int32, (64, b), 0) + start
                    == lax.broadcasted_iota(jnp.int32, (64, b), 1)
                )
                first_re = jnp.where(on, 2.0 * row_re, 0.0) - (scaled_re * row_re - scaled_im * row_im)
                first_im = jnp.where(on, 2.0 * row_im, 0.0) - (scaled_re * row_im + scaled_im * row_re)
                first[rows, 0:b] = first_re
                first[rows, b:] = first_im
                fhat[rows, 0:b] = first_re.astype(BF16)
                fhat[rows, b:] = first_im.astype(BF16)
        expand(fhat)
        for n, w in bands:
            wide[0:b, n : n + w] = dot(sysb[...], fhat[:, n : n + w]).astype(BF16)
        expand(wide)
        for n, w in bands:
            rhat[e, 0:b, n : n + w] = (
                2.0 * first[:, n : n + w] - dot(fhat[0:b, :], wide[:, n : n + w])
            ).astype(BF16)

        @pl.when(slab > 0)
        def _():
            ret_copy(e).start()

        ret_store(e, 0).start()
        ret_store(e, 1).start()
        expand(rhat.at[e])
        for n, w in bands:
            ghat[e, 0:b, n : n + w] = dot(rhat[e, 0:b, :], chat[:, n : n + w]).astype(BF16)
        expand(ghat.at[e])

    def les_stage(e):
        p = ne + e
        pass_on(p)
        arrived(p)

        def make_source(rows):
            for part in range(2):
                wide[rows, part * b : (part + 1) * b] = phonon(p, part, rows).astype(BF16)

        over_rows(make_source)
        expand(wide)
        for n, w in bands:
            mv[:, n : n + w] = dot(rhat[e, 0:b, :], wide[:, n : n + w]).astype(BF16)
        for n, w in bands:
            acc[:, n : n + w] = dot_nt(mv[...], rhat[e, n : n + w, :])

        @pl.when(slab < last)
        def _():
            les_copy(e).wait_recv()

        for n, w, value in congruence(ghat.at[e], bl.at[e]):
            les[e, :, n : n + w] = (acc[:, n : n + w] + value).astype(BF16)

        @pl.when(slab > 0)
        def _():
            les_copy(e).start()

        les_store(e, 0).start()
        les_store(e, 1).start()

    def turn(t, carry):
        @pl.when(t < pieces)
        def _():
            prep(t)

        c = t - LEAD

        @pl.when(jnp.logical_and(c >= 0, c < ne))
        def _():
            ret_stage(c)

        @pl.when(c >= ne)
        def _():
            les_stage(c - ne)

        return carry

    lax.fori_loop(0, pieces + LEAD, turn, 0)

    def drain(p, carry):
        y_copy(p).wait_send()
        either(raw_seam, lambda: raw_half(p).wait_send(), lambda: raw_copy(p).wait_send())
        either(sel_seam, lambda: sel_half(p).wait_send(), lambda: sel_copy(p).wait_send())
        either(raw_seam, lambda: pass_sel(p, parity).wait_send(), nothing)
        either(sel_seam, lambda: pass_raw(p, parity).wait_send(), nothing)
        return carry

    lax.fori_loop(0, pieces, drain, 0)

    def drain_out(e, carry):
        @pl.when(slab > 0)
        def _():
            ret_copy(e).wait_send()
            les_copy(e).wait_send()

        for part in range(2):
            ret_store(e, part).wait()
            les_store(e, part).wait()
        return carry

    lax.fori_loop(0, ne, drain_out, 0)


def body(
    energies, onsite, hamiltonian, hopping, contact, previous, neighbours, mode_index, mode_strength
):
    slabs, points = lax.axis_size("slab"), lax.axis_size("kt")
    ne, b = energies.shape[0], onsite.shape[-1]
    pieces = 2 * ne
    block = (pieces, 2, b, b)
    cat, square = (b, 2 * b), (2 * b, 2 * b)
    smem = pl.BlockSpec(memory_space=pltpu.SMEM)
    vmem = pl.BlockSpec(memory_space=pltpu.VMEM)
    anywhere = pl.BlockSpec(memory_space=pl.ANY)
    dma = pltpu.SemaphoreType.DMA
    table, both_far = pl.pallas_call(
        functools.partial(agree, points, b),
        out_shape=(jax.ShapeDtypeStruct((16, b), F32), jax.ShapeDtypeStruct((1, 1), F32)),
        in_specs=[smem] * 4,
        out_specs=(vmem, smem),
        scratch_shapes=[
            pltpu.VMEM((8, 128), F32),
            pltpu.VMEM((points, 8, 128), F32),
            dma((points,)),
            dma((points,)),
        ],
        compiler_params=pltpu.CompilerParams(collective_id=0, has_side_effects=True),
        name="agree",
    )(energies, neighbours, mode_index, mode_strength)
    out = jax.ShapeDtypeStruct((ne, 2, b, b), BF16)

    def sweep(halve, *operands):
        return pl.pallas_call(
            functools.partial(kernel, halve, slabs, points, ne, b),
            out_shape=(out, out),
            in_specs=[smem] + [vmem] * 5 + [anywhere],
            out_specs=(anywhere, anywhere),
            scratch_shapes=[
                pltpu.VMEM(block, BF16),
                pltpu.VMEM(block, BF16),
                pltpu.VMEM(block, BF16),
                pltpu.VMEM(block, BF16),
                pltpu.VMEM((pieces, b, b) if halve else (1, 16, 128), BF16),
                pltpu.VMEM((ne,) + cat, BF16),
                pltpu.VMEM((ne,) + cat, BF16),
                pltpu.VMEM(square, BF16),
                pltpu.VMEM((ne,) + square, BF16),
                pltpu.VMEM((ne,) + square, BF16),
                pltpu.VMEM((ne,) + cat, BF16),
                pltpu.VMEM(square, BF16),
                pltpu.VMEM(square, BF16),
                pltpu.VMEM(cat, BF16),
                pltpu.VMEM(cat, BF16),
                pltpu.VMEM(cat, F32),
                pltpu.VMEM(cat, F32),
            ]
            + [dma((pieces,))] * 11
            + [dma((pieces, 2))],
            compiler_params=pltpu.CompilerParams(
                collective_id=2 if halve else 1,
                has_side_effects=True,
                vmem_limit_bytes=50 * 1024 * 1024,
            ),
            name="sweep_halved" if halve else "sweep_whole",
        )(*operands)

    retarded, lesser = lax.cond(
        both_far[0, 0] > 0.5,
        functools.partial(sweep, False),
        functools.partial(sweep, True),
        energies, table, onsite[0], hamiltonian[0, 0], hopping[0, 0], contact[0],
        previous.reshape((ne, 2, 2, b, b)),
    )
    whole = (1, ne, 1, 2, b, b)
    return retarded.reshape(whole), lesser.reshape(whole)


def solution(mesh):
    in_specs = (
        P(),
        P("kt", "slab", None),
        P("kt", "slab", None, None, None),
        P("kt", "slab", None, None, None),
        P("kt", None, None, None),
        P("kt", None, "slab", None, None, None, None),
        P("kt", None),
        P("kt", None),
        P(),
    )
    out_specs = (P("kt", None, "slab", None, None, None), P("kt", None, "slab", None, None, None))
    return jax.shard_map(body, mesh=mesh, in_specs=in_specs, out_specs=out_specs, check_vma=False)
```

```python
import functools

import jax
import jax.numpy as jnp
from jax import lax
from jax.experimental import pallas as pl
from jax.experimental.pallas import tpu as pltpu
from jax.sharding import PartitionSpec as P

broaden = 0.05
fermi_level = 0.0
thermal = 0.1

MESH = pl.DeviceIdType.MESH
LEAD = 4
AHEAD = 2
F32 = jnp.float32
BF16 = jnp.bfloat16


def dot(a, b):
    return jnp.dot(a, b, preferred_element_type=F32)


def dot_nt(a, b):
    return lax.dot_general(a, b, (((1,), (1,)), ((), ())), preferred_element_type=F32)


def agree(
    points, b,
    energies, neighbours, mode_index, mode_strength,
    table, both_far,
    mine, every, send, recv,
):
    k = lax.axis_index("kt")
    even = lax.rem(k, 2) == 0
    barrier = pltpu.get_barrier_semaphore()

    def peer(by):
        return {"kt": lax.rem(k + by, points)}

    def greet(by, carry):
        pl.semaphore_signal(barrier, inc=1, device_id=peer(by), device_id_type=MESH)
        return carry

    lax.fori_loop(1, points, greet, 0)
    pl.semaphore_wait(barrier, points - 1)
    left = jnp.where(neighbours[0, 0] == lax.rem(k - 1 + points, points), 1.0, 0.0)
    right = jnp.where(neighbours[0, 1] == lax.rem(k + 1, points), 1.0, 0.0)
    row = lax.broadcasted_iota(jnp.int32, (8, 128), 0)
    mine[...] = jnp.where(row == 0, left, right)
    every[k] = mine[...]

    def tell(by):
        return pltpu.make_async_remote_copy(
            mine, every.at[k], send.at[by], recv.at[k], device_id=peer(by), device_id_type=MESH
        )

    def hear(by):
        j = lax.rem(k + by, points)
        return pltpu.make_async_remote_copy(
            mine, every.at[j], send.at[by], recv.at[j], device_id=peer(by), device_id_type=MESH
        )

    def start(by, carry):
        tell(by).start()
        return carry

    def finish(by, carry):
        tell(by).wait_send()
        hear(by).wait_recv()
        return carry

    lax.fori_loop(1, points, start, 0)
    lax.fori_loop(1, points, finish, 0)

    def near(j):
        j = lax.rem(j + points, points)
        return every[j, 0:1, :], every[j, 1:2, :]

    left_2, right_2 = near(k + 2), near(k - 2)
    left_1, right_1 = near(k + 1), near(k - 1)
    chosen = jnp.where(even, left_2[0], right_2[1])
    wrapped = jnp.where(even, right_1[1], left_1[0])
    strength_left = mode_strength[mode_index[0, 0]]
    strength_right = mode_strength[mode_index[0, 1]]
    weight_sel = jnp.where(even, strength_left, strength_right)
    weight_other = jnp.where(even, strength_right, strength_left)
    other_near = jnp.where(even, right, left)
    full = jnp.zeros((1, 128), F32)
    rows = [
        chosen,
        wrapped,
        full + weight_sel,
        full + weight_other * other_near,
        full + weight_other * (1.0 - other_near),
    ]
    for e in range(energies.shape[0]):
        rows.append(1.0 / (1.0 + jnp.exp((full + energies[e] - fermi_level) / thermal)))
    for i, value in enumerate(rows):
        for start_at in range(0, b, 128):
            table[i : i + 1, start_at : start_at + 128] = value
    up = (1.0 - near(0)[0]) * (1.0 - near(1)[0])
    down = (1.0 - near(points - 1)[1]) * (1.0 - near(points - 2)[1])
    both_far[0, 0] = jnp.max(jnp.maximum(up, down))


def kernel(
    halve, slabs, points, ne, b,
    energies, table, onsite, ham, hop, contact, prev,
    ret_out, les_out,
    own, mate, zsel, zraw, stage, bx, bl, chat, rhat, ghat, les, wide, fhat, mv, sysb, acc, first,
    own_sem, y_send, y_recv, s_send, s_recv, r_send, r_recv, f_send, f_recv, b_send, b_recv, o_sem,
):
    slab = lax.axis_index("slab")
    k = lax.axis_index("kt")
    pieces = 2 * ne
    step = 2 - 4 * lax.rem(k, 2)
    parity = lax.rem(k, 2)
    mate_k = k + 1 - 2 * lax.rem(k, 2)
    sel_k = lax.rem(k + step + points, points)
    raw_k = lax.rem(k - step + points, points)
    raw_seam = jnp.logical_and(halve, jnp.logical_or(k == 0, k == points - 1))
    sel_seam = jnp.logical_and(halve, jnp.logical_or(k == 1, k == points - 2))
    last = slabs - 1
    bands = [(n, min(256, 2 * b - n)) for n in range(0, 2 * b, 256)]
    rows_per = 48

    barrier = pltpu.get_barrier_semaphore()
    for other in (mate_k, sel_k, raw_k):
        pl.semaphore_signal(barrier, inc=1, device_id={"kt": other}, device_id_type=MESH)
    for by in (1, slabs - 1):
        pl.semaphore_signal(
            barrier, inc=1, device_id={"slab": lax.rem(slab + by, slabs)}, device_id_type=MESH
        )
    pl.semaphore_wait(barrier, 5)

    def source(p):
        return prev.at[lax.rem(p, ne), p // ne]

    def y_copy(p):
        return pltpu.make_async_remote_copy(
            source(p), mate.at[p], y_send.at[p], y_recv.at[p],
            device_id={"kt": mate_k}, device_id_type=MESH,
        )

    def raw_copy(p):
        return pltpu.make_async_remote_copy(
            source(p), zraw.at[p], r_send.at[p], r_recv.at[p],
            device_id={"kt": raw_k}, device_id_type=MESH,
        )

    def sel_copy(p):
        return pltpu.make_async_remote_copy(
            own.at[p], zsel.at[p], s_send.at[p], s_recv.at[p],
            device_id={"kt": sel_k}, device_id_type=MESH,
        )

    def own_copy(p):
        return pltpu.make_async_copy(source(p), own.at[p], own_sem.at[p])

    def raw_half(p):
        return pltpu.make_async_remote_copy(
            stage.at[p], zraw.at[p, parity], r_send.at[p], r_recv.at[p],
            device_id={"kt": raw_k}, device_id_type=MESH,
        )

    def sel_half(p):
        return pltpu.make_async_remote_copy(
            stage.at[p], zsel.at[p, parity], s_send.at[p], s_recv.at[p],
            device_id={"kt": sel_k}, device_id_type=MESH,
        )

    def pass_sel(p, part):
        return pltpu.make_async_remote_copy(
            zsel.at[p, part], zraw.at[p, part], f_send.at[p], f_recv.at[p],
            device_id={"kt": mate_k}, device_id_type=MESH,
        )

    def pass_raw(p, part):
        return pltpu.make_async_remote_copy(
            zraw.at[p, part], zsel.at[p, part], f_send.at[p], f_recv.at[p],
            device_id={"kt": mate_k}, device_id_type=MESH,
        )

    def either(seam, half, whole):
        if not halve:
            whole()
            return
        pl.when(seam)(half)
        pl.when(jnp.logical_not(seam))(whole)

    def nothing():
        return None

    def pass_on(p):
        if not halve:
            return

        @pl.when(raw_seam)
        def _():
            sel_half(p).wait_recv()
            pass_sel(p, parity).start()

        @pl.when(sel_seam)
        def _():
            raw_half(p).wait_recv()
            pass_raw(p, parity).start()

    def arrived(p):
        either(raw_seam, lambda: pass_raw(p, 1 - parity).wait_recv(), lambda: sel_copy(p).wait_recv())
        either(sel_seam, lambda: pass_sel(p, 1 - parity).wait_recv(), lambda: raw_copy(p).wait_recv())

    def ret_copy(e):
        return pltpu.make_async_remote_copy(
            rhat.at[e, pl.ds(0, b)], bx.at[e], b_send.at[e], b_recv.at[e],
            device_id={"slab": jnp.maximum(slab - 1, 0)}, device_id_type=MESH,
        )

    def les_copy(e):
        return pltpu.make_async_remote_copy(
            les.at[e], bl.at[e], b_send.at[ne + e], b_recv.at[ne + e],
            device_id={"slab": jnp.maximum(slab - 1, 0)}, device_id_type=MESH,
        )

    def ret_store(e, part):
        return pltpu.make_async_copy(
            rhat.at[e, pl.ds(0, b), pl.ds(part * b, b)], ret_out.at[e, part], o_sem.at[e, part]
        )

    def les_store(e, part):
        return pltpu.make_async_copy(
            les.at[e, :, pl.ds(part * b, b)], les_out.at[e, part], o_sem.at[ne + e, part]
        )

    def begin(p):
        y_copy(p).start()
        own_copy(p).start()

    def begin_raw(p):
        either(raw_seam, nothing, lambda: raw_copy(p).start())

    for p in range(AHEAD):
        begin(p)
    begin_raw(0)

    def expand(ref):
        ref[b:, 0:b] = -ref[0:b, b:]
        ref[b:, b:] = ref[0:b, 0:b]

    chat[0:b, 0:b] = hop[0]
    chat[0:b, b:] = hop[1]
    expand(chat)

    @pl.when(slab == last)
    def _():
        for part in range(2):
            value = contact[part].astype(F32)
            flipped = value.T
            skew = value - flipped if part == 0 else value + flipped
            acc[:, part * b : (part + 1) * b] = skew
            for e in range(ne):
                bx[e, :, part * b : (part + 1) * b] = contact[part]
        for e in range(ne):
            for part in range(2):
                columns = slice(part * b, (part + 1) * b)
                bl[e, :, columns] = (-table[5 + e : 6 + e, :] * acc[:, columns]).astype(BF16)

    def phonon(p, part, rows):
        return (
            table[2:3, :] * zsel[p, part, rows].astype(F32)
            + table[3:4, :] * mate[p, part, rows].astype(F32)
            + table[4:5, :] * zraw[p, part, rows].astype(F32)
        )

    def over_rows(do):
        def one(i, carry):
            do(pl.ds(pl.multiple_of(i * rows_per, rows_per), rows_per))
            return carry

        lax.fori_loop(0, b // rows_per, one, 0)

    def mixed(chosen, p, part, rows):
        return (
            chosen * mate[p, part, rows].astype(F32) + (1.0 - chosen) * own[p, part, rows].astype(F32)
        ).astype(BF16)

    def meet(p):
        y_copy(p).wait_recv()
        own_copy(p).wait()

        if halve:

            @pl.when(jnp.logical_or(raw_seam, sel_seam))
            def _():
                chosen = jnp.where(raw_seam, 1.0 - table[1:2, :], table[0:1, :])

                def pick(rows):
                    stage[p, rows] = mixed(chosen, p, parity, rows)

                over_rows(pick)

            pl.when(raw_seam)(lambda: raw_half(p).start())
            pl.when(sel_seam)(lambda: sel_half(p).start())

        @pl.when(p + AHEAD < pieces)
        def _():
            begin(p + AHEAD)

    def prep(p):
        def pick(rows):
            for part in range(2):
                own[p, part, rows] = mixed(table[0:1, :], p, part, rows)

        def start_sel():
            over_rows(pick)
            sel_copy(p).start()

        either(sel_seam, nothing, start_sel)

        @pl.when(p + 1 < pieces)
        def _():
            begin_raw(p + 1)

    def congruence(left, boundary):
        wide[0:b, :] = boundary[...]
        expand(wide)
        for n, w in bands:
            mv[:, n : n + w] = dot(left[0:b, :], wide[:, n : n + w]).astype(BF16)
        return [(n, w, dot_nt(mv[...], left[n : n + w, :])) for n, w in bands]

    def ret_stage(e):
        @pl.when(slab < last)
        def _():
            ret_copy(e).wait_recv()

        for n, w, value in congruence(chat, bx.at[e]):
            acc[:, n : n + w] = value
        arrived(e)
        energy = energies[e]

        def make_system(rows):
            at = lax.broadcasted_iota(jnp.int32, (rows_per, b), 0) + rows.start
            eye = at == lax.broadcasted_iota(jnp.int32, (rows_per, b), 1)
            real = jnp.where(eye, energy - onsite[...], 0.0)
            imag = jnp.where(eye, broaden, 0.0)
            for part, diagonal in ((0, real), (1, imag)):
                columns = slice(part * b, (part + 1) * b)
                value = (
                    diagonal - ham[part, rows].astype(F32) - acc[rows, columns] - phonon(e, part, rows)
                )
                acc[rows, columns] = value
                sysb[rows, columns] = value.astype(BF16)

        over_rows(make_system)
        eye = lax.broadcasted_iota(jnp.int32, (128, 128), 0) == lax.broadcasted_iota(
            jnp.int32, (128, 128), 1
        )
        across, along = [], []
        for i in range(b // 128):
            rows = slice(i * 128, (i + 1) * 128)
            real = jnp.where(eye, acc[rows, i * 128 : (i + 1) * 128], 0.0)
            imag = jnp.where(eye, acc[rows, b + i * 128 : b + (i + 1) * 128], 0.0)
            for axis, found in ((0, across), (1, along)):
                re = jnp.sum(real, axis=axis, keepdims=True)
                im = jnp.sum(imag, axis=axis, keepdims=True)
                modulus = re * re + im * im
                found.append((re / modulus, -im / modulus))
        row_re = jnp.concatenate([found[0] for found in across], axis=1)
        row_im = jnp.concatenate([found[1] for found in across], axis=1)
        for i in range(b // 128):
            col_re, col_im = along[i]
            for half in range(2):
                start = i * 128 + half * 64
                rows = slice(start, start + 64)
                cre = col_re[half * 64 : half * 64 + 64]
                cim = col_im[half * 64 : half * 64 + 64]
                re, im = acc[rows, 0:b], acc[rows, b:]
                scaled_re = cre * re - cim * im
                scaled_im = cre * im + cim * re
                on = (
                    lax.broadcasted_iota(jnp.int32, (64, b), 0) + start
                    == lax.broadcasted_iota(jnp.int32, (64, b), 1)
                )
                first_re = jnp.where(on, 2.0 * row_re, 0.0) - (scaled_re * row_re - scaled_im * row_im)
                first_im = jnp.where(on, 2.0 * row_im, 0.0) - (scaled_re * row_im + scaled_im * row_re)
                first[rows, 0:b] = first_re
                first[rows, b:] = first_im
                fhat[rows, 0:b] = first_re.astype(BF16)
                fhat[rows, b:] = first_im.astype(BF16)
        expand(fhat)
        for n, w in bands:
            wide[0:b, n : n + w] = dot(sysb[...], fhat[:, n : n + w]).astype(BF16)
        expand(wide)
        for n, w in bands:
            rhat[e, 0:b, n : n + w] = (
                2.0 * first[:, n : n + w] - dot(fhat[0:b, :], wide[:, n : n + w])
            ).astype(BF16)

        @pl.when(slab > 0)
        def _():
            ret_copy(e).start()

        ret_store(e, 0).start()
        ret_store(e, 1).start()
        expand(rhat.at[e])
        for n, w in bands:
            ghat[e, 0:b, n : n + w] = dot(rhat[e, 0:b, :], chat[:, n : n + w]).astype(BF16)
        expand(ghat.at[e])

    def les_stage(e):
        p = ne + e
        arrived(p)

        def make_source(rows):
            for part in range(2):
                wide[rows, part * b : (part + 1) * b] = phonon(p, part, rows).astype(BF16)

        over_rows(make_source)
        expand(wide)
        for n, w in bands:
            mv[:, n : n + w] = dot(rhat[e, 0:b, :], wide[:, n : n + w]).astype(BF16)
        for n, w in bands:
            acc[:, n : n + w] = dot_nt(mv[...], rhat[e, n : n + w, :])

        @pl.when(slab < last)
        def _():
            les_copy(e).wait_recv()

        for n, w, value in congruence(ghat.at[e], bl.at[e]):
            les[e, :, n : n + w] = (acc[:, n : n + w] + value).astype(BF16)

        @pl.when(slab > 0)
        def _():
            les_copy(e).start()

        les_store(e, 0).start()
        les_store(e, 1).start()

    def turn(t, carry):
        @pl.when(t < pieces)
        def _():
            meet(t)

        ready = t - 1 if halve else t

        @pl.when(jnp.logical_and(ready >= 0, ready < pieces))
        def _():
            prep(ready)

        c = t - LEAD

        @pl.when(jnp.logical_and(c + 1 >= 0, c + 1 < pieces))
        def _():
            pass_on(c + 1)

        @pl.when(jnp.logical_and(c >= 0, c < ne))
        def _():
            ret_stage(c)

        @pl.when(c >= ne)
        def _():
            les_stage(c - ne)

        return carry

    lax.fori_loop(0, pieces + LEAD, turn, 0)

    def drain(p, carry):
        y_copy(p).wait_send()
        either(raw_seam, lambda: raw_half(p).wait_send(), lambda: raw_copy(p).wait_send())
        either(sel_seam, lambda: sel_half(p).wait_send(), lambda: sel_copy(p).wait_send())
        either(raw_seam, lambda: pass_sel(p, parity).wait_send(), nothing)
        either(sel_seam, lambda: pass_raw(p, parity).wait_send(), nothing)
        return carry

    lax.fori_loop(0, pieces, drain, 0)

    def drain_out(e, carry):
        @pl.when(slab > 0)
        def _():
            ret_copy(e).wait_send()
            les_copy(e).wait_send()

        for part in range(2):
            ret_store(e, part).wait()
            les_store(e, part).wait()
        return carry

    lax.fori_loop(0, ne, drain_out, 0)


def body(
    energies, onsite, hamiltonian, hopping, contact, previous, neighbours, mode_index, mode_strength
):
    slabs, points = lax.axis_size("slab"), lax.axis_size("kt")
    ne, b = energies.shape[0], onsite.shape[-1]
    pieces = 2 * ne
    block = (pieces, 2, b, b)
    cat, square = (b, 2 * b), (2 * b, 2 * b)
    smem = pl.BlockSpec(memory_space=pltpu.SMEM)
    vmem = pl.BlockSpec(memory_space=pltpu.VMEM)
    anywhere = pl.BlockSpec(memory_space=pl.ANY)
    dma = pltpu.SemaphoreType.DMA
    table, both_far = pl.pallas_call(
        functools.partial(agree, points, b),
        out_shape=(jax.ShapeDtypeStruct((16, b), F32), jax.ShapeDtypeStruct((1, 1), F32)),
        in_specs=[smem] * 4,
        out_specs=(vmem, smem),
        scratch_shapes=[
            pltpu.VMEM((8, 128), F32),
            pltpu.VMEM((points, 8, 128), F32),
            dma((points,)),
            dma((points,)),
        ],
        compiler_params=pltpu.CompilerParams(collective_id=0, has_side_effects=True),
        name="agree",
    )(energies, neighbours, mode_index, mode_strength)
    out = jax.ShapeDtypeStruct((ne, 2, b, b), BF16)

    def sweep(halve, *operands):
        return pl.pallas_call(
            functools.partial(kernel, halve, slabs, points, ne, b),
            out_shape=(out, out),
            in_specs=[smem] + [vmem] * 5 + [anywhere],
            out_specs=(anywhere, anywhere),
            scratch_shapes=[
                pltpu.VMEM(block, BF16),
                pltpu.VMEM(block, BF16),
                pltpu.VMEM(block, BF16),
                pltpu.VMEM(block, BF16),
                pltpu.VMEM((pieces, b, b) if halve else (1, 16, 128), BF16),
                pltpu.VMEM((ne,) + cat, BF16),
                pltpu.VMEM((ne,) + cat, BF16),
                pltpu.VMEM(square, BF16),
                pltpu.VMEM((ne,) + square, BF16),
                pltpu.VMEM((ne,) + square, BF16),
                pltpu.VMEM((ne,) + cat, BF16),
                pltpu.VMEM(square, BF16),
                pltpu.VMEM(square, BF16),
                pltpu.VMEM(cat, BF16),
                pltpu.VMEM(cat, BF16),
                pltpu.VMEM(cat, F32),
                pltpu.VMEM(cat, F32),
            ]
            + [dma((pieces,))] * 11
            + [dma((pieces, 2))],
            compiler_params=pltpu.CompilerParams(
                collective_id=2 if halve else 1,
                has_side_effects=True,
                vmem_limit_bytes=50 * 1024 * 1024,
            ),
            name="sweep_halved" if halve else "sweep_whole",
        )(*operands)

    retarded, lesser = lax.cond(
        both_far[0, 0] > 0.5,
        functools.partial(sweep, False),
        functools.partial(sweep, True),
        energies, table, onsite[0], hamiltonian[0, 0], hopping[0, 0], contact[0],
        previous.reshape((ne, 2, 2, b, b)),
    )
    whole = (1, ne, 1, 2, b, b)
    return retarded.reshape(whole), lesser.reshape(whole)


def solution(mesh):
    in_specs = (
        P(),
        P("kt", "slab", None),
        P("kt", "slab", None, None, None),
        P("kt", "slab", None, None, None),
        P("kt", None, None, None),
        P("kt", None, "slab", None, None, None, None),
        P("kt", None),
        P("kt", None),
        P(),
    )
    out_specs = (P("kt", None, "slab", None, None, None), P("kt", None, "slab", None, None, None))
    return jax.shard_map(body, mesh=mesh, in_specs=in_specs, out_specs=out_specs, check_vma=False)
```

```python
import functools

import jax
import jax.numpy as jnp
from jax import lax
from jax.experimental import pallas as pl
from jax.experimental.pallas import tpu as pltpu
from jax.sharding import PartitionSpec as P

broaden = 0.05
fermi_level = 0.0
thermal = 0.1

MESH = pl.DeviceIdType.MESH
LEAD = 4
AHEAD = 2
F32 = jnp.float32
BF16 = jnp.bfloat16


def dot(a, b):
    return jnp.dot(a, b, preferred_element_type=F32)


def dot_nt(a, b):
    return lax.dot_general(a, b, (((1,), (1,)), ((), ())), preferred_element_type=F32)


def agree(
    points, b,
    energies, neighbours, mode_index, mode_strength,
    table, both_far,
    mine, every, send, recv,
):
    k = lax.axis_index("kt")
    even = lax.rem(k, 2) == 0
    barrier = pltpu.get_barrier_semaphore()

    def peer(by):
        return {"kt": lax.rem(k + by, points)}

    def greet(by, carry):
        pl.semaphore_signal(barrier, inc=1, device_id=peer(by), device_id_type=MESH)
        return carry

    lax.fori_loop(1, points, greet, 0)
    pl.semaphore_wait(barrier, points - 1)
    left = jnp.where(neighbours[0, 0] == lax.rem(k - 1 + points, points), 1.0, 0.0)
    right = jnp.where(neighbours[0, 1] == lax.rem(k + 1, points), 1.0, 0.0)
    row = lax.broadcasted_iota(jnp.int32, (8, 128), 0)
    mine[...] = jnp.where(row == 0, left, right)
    every[k] = mine[...]

    def tell(by):
        return pltpu.make_async_remote_copy(
            mine, every.at[k], send.at[by], recv.at[k], device_id=peer(by), device_id_type=MESH
        )

    def hear(by):
        j = lax.rem(k + by, points)
        return pltpu.make_async_remote_copy(
            mine, every.at[j], send.at[by], recv.at[j], device_id=peer(by), device_id_type=MESH
        )

    def start(by, carry):
        tell(by).start()
        return carry

    def finish(by, carry):
        tell(by).wait_send()
        hear(by).wait_recv()
        return carry

    lax.fori_loop(1, points, start, 0)
    lax.fori_loop(1, points, finish, 0)

    def near(j):
        j = lax.rem(j + points, points)
        return every[j, 0:1, :], every[j, 1:2, :]

    left_2, right_2 = near(k + 2), near(k - 2)
    left_1, right_1 = near(k + 1), near(k - 1)
    chosen = jnp.where(even, left_2[0], right_2[1])
    wrapped = jnp.where(even, right_1[1], left_1[0])
    strength_left = mode_strength[mode_index[0, 0]]
    strength_right = mode_strength[mode_index[0, 1]]
    weight_sel = jnp.where(even, strength_left, strength_right)
    weight_other = jnp.where(even, strength_right, strength_left)
    other_near = jnp.where(even, right, left)
    full = jnp.zeros((1, 128), F32)
    rows = [
        chosen,
        wrapped,
        full + weight_sel,
        full + weight_other * other_near,
        full + weight_other * (1.0 - other_near),
    ]
    for e in range(energies.shape[0]):
        rows.append(1.0 / (1.0 + jnp.exp((full + energies[e] - fermi_level) / thermal)))
    for i, value in enumerate(rows):
        for start_at in range(0, b, 128):
            table[i : i + 1, start_at : start_at + 128] = value
    up = (1.0 - near(0)[0]) * (1.0 - near(1)[0])
    down = (1.0 - near(points - 1)[1]) * (1.0 - near(points - 2)[1])
    both_far[0, 0] = jnp.max(jnp.maximum(up, down))


def kernel(
    halve, slabs, points, ne, b,
    energies, table, onsite, ham, hop, contact, prev,
    ret_out, les_out,
    own, mate, zsel, zraw, stage, bx, bl, chat, rhat, ghat, les, wide, fhat, mv, sysb, acc, first,
    own_sem, y_send, y_recv, s_send, s_recv, r_send, r_recv, f_send, f_recv, b_send, b_recv, o_sem,
    u_send, u_recv, v_send, v_recv,
):
    slab = lax.axis_index("slab")
    k = lax.axis_index("kt")
    pieces = 2 * ne
    step = 2 - 4 * lax.rem(k, 2)
    parity = lax.rem(k, 2)
    mate_k = k + 1 - 2 * lax.rem(k, 2)
    sel_k = lax.rem(k + step + points, points)
    raw_k = lax.rem(k - step + points, points)
    raw_seam = jnp.logical_and(halve, jnp.logical_or(k == 0, k == points - 1))
    sel_seam = jnp.logical_and(halve, jnp.logical_or(k == 1, k == points - 2))
    last = slabs - 1
    bands = [(n, min(256, 2 * b - n)) for n in range(0, 2 * b, 256)]
    rows_per = 48

    barrier = pltpu.get_barrier_semaphore()
    for other in (mate_k, sel_k, raw_k):
        pl.semaphore_signal(barrier, inc=1, device_id={"kt": other}, device_id_type=MESH)
    for by in (1, slabs - 1):
        pl.semaphore_signal(
            barrier, inc=1, device_id={"slab": lax.rem(slab + by, slabs)}, device_id_type=MESH
        )
    pl.semaphore_wait(barrier, 5)

    def source(p):
        return prev.at[lax.rem(p, ne), p // ne]

    def y_copy(p):
        return pltpu.make_async_remote_copy(
            source(p), mate.at[p], y_send.at[p], y_recv.at[p],
            device_id={"kt": mate_k}, device_id_type=MESH,
        )

    def raw_copy(p):
        return pltpu.make_async_remote_copy(
            source(p), zraw.at[p], r_send.at[p], r_recv.at[p],
            device_id={"kt": raw_k}, device_id_type=MESH,
        )

    def sel_copy(p):
        return pltpu.make_async_remote_copy(
            own.at[p], zsel.at[p], s_send.at[p], s_recv.at[p],
            device_id={"kt": sel_k}, device_id_type=MESH,
        )

    units = 2 * (b // 128)

    def unit(i, part):
        part = part if i < units // 2 else 1 - part
        return 0, part, pl.ds((i % (units // 2)) * 128, 128)

    def y_unit(i, part):
        return pltpu.make_async_remote_copy(
            prev.at[0].at[unit(i, part)], mate.at[unit(i, part)], u_send.at[i], u_recv.at[i],
            device_id={"kt": mate_k}, device_id_type=MESH,
        )

    def sel_unit(i):
        return pltpu.make_async_remote_copy(
            own.at[unit(i, parity)], zsel.at[unit(i, parity)], v_send.at[i], v_recv.at[i],
            device_id={"kt": sel_k}, device_id_type=MESH,
        )

    def wait_sel(p):
        @pl.when(p == 0)
        def _():
            for i in range(units):
                sel_unit(i).wait_recv()

        @pl.when(p > 0)
        def _():
            sel_copy(p).wait_recv()

    def own_copy(p):
        return pltpu.make_async_copy(source(p), own.at[p], own_sem.at[p])

    def raw_half(p):
        return pltpu.make_async_remote_copy(
            stage.at[p], zraw.at[p, parity], r_send.at[p], r_recv.at[p],
            device_id={"kt": raw_k}, device_id_type=MESH,
        )

    def sel_half(p):
        return pltpu.make_async_remote_copy(
            stage.at[p], zsel.at[p, parity], s_send.at[p], s_recv.at[p],
            device_id={"kt": sel_k}, device_id_type=MESH,
        )

    def pass_sel(p, part):
        return pltpu.make_async_remote_copy(
            zsel.at[p, part], zraw.at[p, part], f_send.at[p], f_recv.at[p],
            device_id={"kt": mate_k}, device_id_type=MESH,
        )

    def pass_raw(p, part):
        return pltpu.make_async_remote_copy(
            zraw.at[p, part], zsel.at[p, part], f_send.at[p], f_recv.at[p],
            device_id={"kt": mate_k}, device_id_type=MESH,
        )

    def either(seam, half, whole):
        if not halve:
            whole()
            return
        pl.when(seam)(half)
        pl.when(jnp.logical_not(seam))(whole)

    def nothing():
        return None

    def pass_on(p):
        if not halve:
            return

        @pl.when(raw_seam)
        def _():
            sel_half(p).wait_recv()
            pass_sel(p, parity).start()

        @pl.when(sel_seam)
        def _():
            raw_half(p).wait_recv()
            pass_raw(p, parity).start()

    def arrived(p):
        either(raw_seam, lambda: pass_raw(p, 1 - parity).wait_recv(), lambda: wait_sel(p))
        either(sel_seam, lambda: pass_sel(p, 1 - parity).wait_recv(), lambda: raw_copy(p).wait_recv())

    def ret_copy(e):
        return pltpu.make_async_remote_copy(
            rhat.at[e, pl.ds(0, b)], bx.at[e], b_send.at[e], b_recv.at[e],
            device_id={"slab": jnp.maximum(slab - 1, 0)}, device_id_type=MESH,
        )

    def les_copy(e):
        return pltpu.make_async_remote_copy(
            les.at[e], bl.at[e], b_send.at[ne + e], b_recv.at[ne + e],
            device_id={"slab": jnp.maximum(slab - 1, 0)}, device_id_type=MESH,
        )

    def ret_store(e, part):
        return pltpu.make_async_copy(
            rhat.at[e, pl.ds(0, b), pl.ds(part * b, b)], ret_out.at[e, part], o_sem.at[e, part]
        )

    def les_store(e, part):
        return pltpu.make_async_copy(
            les.at[e, :, pl.ds(part * b, b)], les_out.at[e, part], o_sem.at[ne + e, part]
        )

    def begin(p):
        y_copy(p).start()
        own_copy(p).start()

    def begin_raw(p):
        either(raw_seam, nothing, lambda: raw_copy(p).start())

    for i in range(units):
        y_unit(i, 1 - parity).start()
    own_copy(0).start()
    begin_raw(0)
    for p in range(1, AHEAD):
        begin(p)

    def expand(ref):
        ref[b:, 0:b] = -ref[0:b, b:]
        ref[b:, b:] = ref[0:b, 0:b]

    chat[0:b, 0:b] = hop[0]
    chat[0:b, b:] = hop[1]
    expand(chat)

    @pl.when(slab == last)
    def _():
        for part in range(2):
            value = contact[part].astype(F32)
            flipped = value.T
            skew = value - flipped if part == 0 else value + flipped
            acc[:, part * b : (part + 1) * b] = skew
            for e in range(ne):
                bx[e, :, part * b : (part + 1) * b] = contact[part]
        for e in range(ne):
            for part in range(2):
                columns = slice(part * b, (part + 1) * b)
                bl[e, :, columns] = (-table[5 + e : 6 + e, :] * acc[:, columns]).astype(BF16)

    def phonon(p, part, rows):
        return (
            table[2:3, :] * zsel[p, part, rows].astype(F32)
            + table[3:4, :] * mate[p, part, rows].astype(F32)
            + table[4:5, :] * zraw[p, part, rows].astype(F32)
        )

    def over_rows(do):
        def one(i, carry):
            do(pl.ds(pl.multiple_of(i * rows_per, rows_per), rows_per))
            return carry

        lax.fori_loop(0, b // rows_per, one, 0)

    def mixed(chosen, p, part, rows):
        return (
            chosen * mate[p, part, rows].astype(F32) + (1.0 - chosen) * own[p, part, rows].astype(F32)
        ).astype(BF16)

    def seam_choice():
        return jnp.where(raw_seam, 1.0 - table[1:2, :], table[0:1, :])

    def start_seam(p):
        pl.when(raw_seam)(lambda: raw_half(p).start())
        pl.when(sel_seam)(lambda: sel_half(p).start())

    def meet_first():
        own_copy(0).wait()
        for i in range(units):
            y_unit(i, parity).wait_recv()
            _, part, rows = unit(i, parity)
            if halve and i < units // 2:

                @pl.when(jnp.logical_or(raw_seam, sel_seam))
                def _():
                    stage[0, rows] = mixed(seam_choice(), 0, part, rows)
                    if i == units // 2 - 1:
                        start_seam(0)

            def start_sel():
                own[0, part, rows] = mixed(table[0:1, :], 0, part, rows)
                sel_unit(i).start()

            either(sel_seam, nothing, start_sel)
        begin(AHEAD)

    def meet(p):
        y_copy(p).wait_recv()
        own_copy(p).wait()

        if halve:

            @pl.when(jnp.logical_or(raw_seam, sel_seam))
            def _():
                chosen = seam_choice()

                def pick(rows):
                    stage[p, rows] = mixed(chosen, p, parity, rows)

                over_rows(pick)
                start_seam(p)

        begin_raw(p)

        @pl.when(p + AHEAD < pieces)
        def _():
            begin(p + AHEAD)

    def prep(p):
        def pick(rows):
            for part in range(2):
                own[p, part, rows] = mixed(table[0:1, :], p, part, rows)

        def start_sel():
            over_rows(pick)
            sel_copy(p).start()

        either(sel_seam, nothing, start_sel)

    def congruence(left, boundary):
        wide[0:b, :] = boundary[...]
        expand(wide)
        for n, w in bands:
            mv[:, n : n + w] = dot(left[0:b, :], wide[:, n : n + w]).astype(BF16)
        return [(n, w, dot_nt(mv[...], left[n : n + w, :])) for n, w in bands]

    def ret_stage(e):
        @pl.when(slab < last)
        def _():
            ret_copy(e).wait_recv()

        for n, w, value in congruence(chat, bx.at[e]):
            acc[:, n : n + w] = value
        arrived(e)
        energy = energies[e]

        def make_system(rows):
            at = lax.broadcasted_iota(jnp.int32, (rows_per, b), 0) + rows.start
            eye = at == lax.broadcasted_iota(jnp.int32, (rows_per, b), 1)
            real = jnp.where(eye, energy - onsite[...], 0.0)
            imag = jnp.where(eye, broaden, 0.0)
            for part, diagonal in ((0, real), (1, imag)):
                columns = slice(part * b, (part + 1) * b)
                value = (
                    diagonal - ham[part, rows].astype(F32) - acc[rows, columns] - phonon(e, part, rows)
                )
                acc[rows, columns] = value
                sysb[rows, columns] = value.astype(BF16)

        over_rows(make_system)
        eye = lax.broadcasted_iota(jnp.int32, (128, 128), 0) == lax.broadcasted_iota(
            jnp.int32, (128, 128), 1
        )
        across, along = [], []
        for i in range(b // 128):
            rows = slice(i * 128, (i + 1) * 128)
            real = jnp.where(eye, acc[rows, i * 128 : (i + 1) * 128], 0.0)
            imag = jnp.where(eye, acc[rows, b + i * 128 : b + (i + 1) * 128], 0.0)
            for axis, found in ((0, across), (1, along)):
                re = jnp.sum(real, axis=axis, keepdims=True)
                im = jnp.sum(imag, axis=axis, keepdims=True)
                modulus = re * re + im * im
                found.append((re / modulus, -im / modulus))
        row_re = jnp.concatenate([found[0] for found in across], axis=1)
        row_im = jnp.concatenate([found[1] for found in across], axis=1)
        for i in range(b // 128):
            col_re, col_im = along[i]
            for half in range(2):
                start = i * 128 + half * 64
                rows = slice(start, start + 64)
                cre = col_re[half * 64 : half * 64 + 64]
                cim = col_im[half * 64 : half * 64 + 64]
                re, im = acc[rows, 0:b], acc[rows, b:]
                scaled_re = cre * re - cim * im
                scaled_im = cre * im + cim * re
                on = (
                    lax.broadcasted_iota(jnp.int32, (64, b), 0) + start
                    == lax.broadcasted_iota(jnp.int32, (64, b), 1)
                )
                first_re = jnp.where(on, 2.0 * row_re, 0.0) - (scaled_re * row_re - scaled_im * row_im)
                first_im = jnp.where(on, 2.0 * row_im, 0.0) - (scaled_re * row_im + scaled_im * row_re)
                first[rows, 0:b] = first_re
                first[rows, b:] = first_im
                fhat[rows, 0:b] = first_re.astype(BF16)
                fhat[rows, b:] = first_im.astype(BF16)
        expand(fhat)
        for n, w in bands:
            wide[0:b, n : n + w] = dot(sysb[...], fhat[:, n : n + w]).astype(BF16)
        expand(wide)
        for n, w in bands:
            rhat[e, 0:b, n : n + w] = (
                2.0 * first[:, n : n + w] - dot(fhat[0:b, :], wide[:, n : n + w])
            ).astype(BF16)

        @pl.when(slab > 0)
        def _():
            ret_copy(e).start()

        ret_store(e, 0).start()
        ret_store(e, 1).start()
        expand(rhat.at[e])
        for n, w in bands:
            ghat[e, 0:b, n : n + w] = dot(rhat[e, 0:b, :], chat[:, n : n + w]).astype(BF16)
        expand(ghat.at[e])

    def les_stage(e):
        p = ne + e

        def from_phonon():
            arrived(p)

            def make_source(rows):
                for part in range(2):
                    wide[rows, part * b : (part + 1) * b] = phonon(p, part, rows).astype(BF16)

            over_rows(make_source)
            expand(wide)
            for n, w in bands:
                mv[:, n : n + w] = dot(rhat[e, 0:b, :], wide[:, n : n + w]).astype(BF16)
            return [(n, w, dot_nt(mv[...], rhat[e, n : n + w, :])) for n, w in bands]

        def both(one, other):
            for n, w, value in one():
                acc[:, n : n + w] = value
            for n, w, value in other():
                les[e, :, n : n + w] = (acc[:, n : n + w] + value).astype(BF16)

        def from_boundary():
            return congruence(ghat.at[e], bl.at[e])

        def from_next_slab():
            les_copy(e).wait_recv()
            return from_boundary()

        pl.when(slab == last)(lambda: both(from_boundary, from_phonon))
        pl.when(slab < last)(lambda: both(from_phonon, from_next_slab))

        @pl.when(slab > 0)
        def _():
            les_copy(e).start()

        les_store(e, 0).start()
        les_store(e, 1).start()

    def turn(t, carry):
        @pl.when(jnp.logical_and(t >= 1, t < pieces))
        def _():
            prep(t)

        @pl.when(t + 1 < pieces)
        def _():
            meet(t + 1)

        c = t - LEAD

        @pl.when(jnp.logical_and(c + 1 >= 0, c + 1 < pieces))
        def _():
            pass_on(c + 1)

        @pl.when(jnp.logical_and(c >= 0, c < ne))
        def _():
            ret_stage(c)

        @pl.when(c >= ne)
        def _():
            les_stage(c - ne)

        return carry

    meet_first()
    lax.fori_loop(0, pieces + LEAD, turn, 0)

    for i in range(units):
        y_unit(i, 1 - parity).wait_send()
        either(sel_seam, nothing, lambda: sel_unit(i).wait_send())

    def drain(p, carry):
        @pl.when(p > 0)
        def _():
            y_copy(p).wait_send()
            either(sel_seam, nothing, lambda: sel_copy(p).wait_send())

        either(raw_seam, lambda: raw_half(p).wait_send(), lambda: raw_copy(p).wait_send())
        either(sel_seam, lambda: sel_half(p).wait_send(), nothing)
        either(raw_seam, lambda: pass_sel(p, parity).wait_send(), nothing)
        either(sel_seam, lambda: pass_raw(p, parity).wait_send(), nothing)
        return carry

    lax.fori_loop(0, pieces, drain, 0)

    def drain_out(e, carry):
        @pl.when(slab > 0)
        def _():
            ret_copy(e).wait_send()
            les_copy(e).wait_send()

        for part in range(2):
            ret_store(e, part).wait()
            les_store(e, part).wait()
        return carry

    lax.fori_loop(0, ne, drain_out, 0)


def body(
    energies, onsite, hamiltonian, hopping, contact, previous, neighbours, mode_index, mode_strength
):
    slabs, points = lax.axis_size("slab"), lax.axis_size("kt")
    ne, b = energies.shape[0], onsite.shape[-1]
    pieces = 2 * ne
    block = (pieces, 2, b, b)
    cat, square = (b, 2 * b), (2 * b, 2 * b)
    smem = pl.BlockSpec(memory_space=pltpu.SMEM)
    vmem = pl.BlockSpec(memory_space=pltpu.VMEM)
    anywhere = pl.BlockSpec(memory_space=pl.ANY)
    dma = pltpu.SemaphoreType.DMA
    table, both_far = pl.pallas_call(
        functools.partial(agree, points, b),
        out_shape=(jax.ShapeDtypeStruct((16, b), F32), jax.ShapeDtypeStruct((1, 1), F32)),
        in_specs=[smem] * 4,
        out_specs=(vmem, smem),
        scratch_shapes=[
            pltpu.VMEM((8, 128), F32),
            pltpu.VMEM((points, 8, 128), F32),
            dma((points,)),
            dma((points,)),
        ],
        compiler_params=pltpu.CompilerParams(collective_id=0, has_side_effects=True),
        name="agree",
    )(energies, neighbours, mode_index, mode_strength)
    out = jax.ShapeDtypeStruct((ne, 2, b, b), BF16)

    def sweep(halve, *operands):
        return pl.pallas_call(
            functools.partial(kernel, halve, slabs, points, ne, b),
            out_shape=(out, out),
            in_specs=[smem] + [vmem] * 5 + [anywhere],
            out_specs=(anywhere, anywhere),
            scratch_shapes=[
                pltpu.VMEM(block, BF16),
                pltpu.VMEM(block, BF16),
                pltpu.VMEM(block, BF16),
                pltpu.VMEM(block, BF16),
                pltpu.VMEM((pieces, b, b) if halve else (1, 16, 128), BF16),
                pltpu.VMEM((ne,) + cat, BF16),
                pltpu.VMEM((ne,) + cat, BF16),
                pltpu.VMEM(square, BF16),
                pltpu.VMEM((ne,) + square, BF16),
                pltpu.VMEM((ne,) + square, BF16),
                pltpu.VMEM((ne,) + cat, BF16),
                pltpu.VMEM(square, BF16),
                pltpu.VMEM(square, BF16),
                pltpu.VMEM(cat, BF16),
                pltpu.VMEM(cat, BF16),
                pltpu.VMEM(cat, F32),
                pltpu.VMEM(cat, F32),
            ]
            + [dma((pieces,))] * 11
            + [dma((pieces, 2))]
            + [dma((2 * (b // 128),))] * 4,
            compiler_params=pltpu.CompilerParams(
                collective_id=2 if halve else 1,
                has_side_effects=True,
                vmem_limit_bytes=50 * 1024 * 1024,
            ),
            name="sweep_halved" if halve else "sweep_whole",
        )(*operands)

    retarded, lesser = lax.cond(
        both_far[0, 0] > 0.5,
        functools.partial(sweep, False),
        functools.partial(sweep, True),
        energies, table, onsite[0], hamiltonian[0, 0], hopping[0, 0], contact[0],
        previous.reshape((ne, 2, 2, b, b)),
    )
    whole = (1, ne, 1, 2, b, b)
    return retarded.reshape(whole), lesser.reshape(whole)


def solution(mesh):
    in_specs = (
        P(),
        P("kt", "slab", None),
        P("kt", "slab", None, None, None),
        P("kt", "slab", None, None, None),
        P("kt", None, None, None),
        P("kt", None, "slab", None, None, None, None),
        P("kt", None),
        P("kt", None),
        P(),
    )
    out_specs = (P("kt", None, "slab", None, None, None), P("kt", None, "slab", None, None, None))
    return jax.shard_map(body, mesh=mesh, in_specs=in_specs, out_specs=out_specs, check_vma=False)
```

```python
import functools

import jax
import jax.numpy as jnp
from jax import lax
from jax.experimental import pallas as pl
from jax.experimental.pallas import tpu as pltpu
from jax.sharding import PartitionSpec as P

broaden = 0.05
fermi_level = 0.0
thermal = 0.1

MESH = pl.DeviceIdType.MESH
LEAD = 4
AHEAD = 2
F32 = jnp.float32
BF16 = jnp.bfloat16


def dot(a, b):
    return jnp.dot(a, b, preferred_element_type=F32)


def dot_nt(a, b):
    return lax.dot_general(a, b, (((1,), (1,)), ((), ())), preferred_element_type=F32)


def agree(
    points, b,
    energies, neighbours, mode_index, mode_strength,
    table, plan,
    mine, every, send, recv,
):
    k = lax.axis_index("kt")
    even = lax.rem(k, 2) == 0
    barrier = pltpu.get_barrier_semaphore()

    def peer(by):
        return {"kt": lax.rem(k + by, points)}

    def greet(by, carry):
        pl.semaphore_signal(barrier, inc=1, device_id=peer(by), device_id_type=MESH)
        return carry

    lax.fori_loop(1, points, greet, 0)
    pl.semaphore_wait(barrier, points - 1)
    left = jnp.where(neighbours[0, 0] == lax.rem(k - 1 + points, points), 1.0, 0.0)
    right = jnp.where(neighbours[0, 1] == lax.rem(k + 1, points), 1.0, 0.0)
    row = lax.broadcasted_iota(jnp.int32, (8, 128), 0)
    mine[...] = jnp.where(row == 0, left, right)
    every[k] = mine[...]

    def tell(by):
        return pltpu.make_async_remote_copy(
            mine, every.at[k], send.at[by], recv.at[k], device_id=peer(by), device_id_type=MESH
        )

    def hear(by):
        j = lax.rem(k + by, points)
        return pltpu.make_async_remote_copy(
            mine, every.at[j], send.at[by], recv.at[j], device_id=peer(by), device_id_type=MESH
        )

    def start(by, carry):
        tell(by).start()
        return carry

    def finish(by, carry):
        tell(by).wait_send()
        hear(by).wait_recv()
        return carry

    lax.fori_loop(1, points, start, 0)
    lax.fori_loop(1, points, finish, 0)

    def near(j):
        j = lax.rem(j + points, points)
        return every[j, 0:1, :], every[j, 1:2, :]

    left_2, right_2 = near(k + 2), near(k - 2)
    left_1, right_1 = near(k + 1), near(k - 1)
    chosen = jnp.where(even, left_2[0], right_2[1])
    wrapped = jnp.where(even, right_1[1], left_1[0])
    strength_left = mode_strength[mode_index[0, 0]]
    strength_right = mode_strength[mode_index[0, 1]]
    weight_sel = jnp.where(even, strength_left, strength_right)
    weight_other = jnp.where(even, strength_right, strength_left)
    other_near = jnp.where(even, right, left)
    full = jnp.zeros((1, 128), F32)
    rows = [
        chosen,
        wrapped,
        full + weight_sel,
        full + weight_other * other_near,
        full + weight_other * (1.0 - other_near),
    ]
    for e in range(energies.shape[0]):
        rows.append(1.0 / (1.0 + jnp.exp((full + energies[e] - fermi_level) / thermal)))
    for i, value in enumerate(rows):
        for start_at in range(0, b, 128):
            table[i : i + 1, start_at : start_at + 128] = value

    def pair_far(m):
        first, second = near(2 * m), near(2 * m + 1)
        return (1.0 - first[0]) * (1.0 - second[0]), (1.0 - first[1]) * (1.0 - second[1])

    def gather(m, found):
        up, down = pair_far(m)
        return jnp.maximum(found[0], up), jnp.maximum(found[1], down)

    up, down = lax.fori_loop(0, points // 2, gather, (full, full))
    seam = jnp.maximum(pair_far(0)[0], pair_far(points // 2 - 1)[1])
    plan[0, 0] = jnp.max(1.0 - seam + seam * (2.0 * (1.0 - down) + down * 3.0 * (1.0 - up)))


WHOLE, SEAM, DOWN, UP = range(4)


def kernel(
    plan, slabs, points, ne, b,
    energies, table, onsite, ham, hop, contact, prev,
    ret_out, les_out,
    own, mate, zsel, zraw, stage, bx, bl, chat, rhat, ghat, les, wide, fhat, mv, sysb, acc, first,
    own_sem, y_send, y_recv, s_send, s_recv, r_send, r_recv, f_send, f_recv, b_send, b_recv, o_sem,
    u_send, u_recv, v_send, v_recv,
):
    slab = lax.axis_index("slab")
    k = lax.axis_index("kt")
    pieces = 2 * ne
    step = 2 - 4 * lax.rem(k, 2)
    parity = lax.rem(k, 2)
    mate_k = k + 1 - 2 * lax.rem(k, 2)
    sel_k = lax.rem(k + step + points, points)
    raw_k = lax.rem(k - step + points, points)
    halve = plan != WHOLE
    even = parity == 0
    odd = parity == 1
    if plan == SEAM:
        raw_cut = jnp.logical_or(k == 0, k == points - 1)
        sel_cut = jnp.logical_or(k == 1, k == points - 2)
        raw_got, sel_got = sel_cut, raw_cut
    elif plan == DOWN:
        raw_cut, sel_cut, raw_got, sel_got = even, odd, even, odd
    else:
        raw_cut, sel_cut, raw_got, sel_got = odd, even, odd, even
    last = slabs - 1
    bands = [(n, min(256, 2 * b - n)) for n in range(0, 2 * b, 256)]
    rows_per = 48

    barrier = pltpu.get_barrier_semaphore()
    for other in (mate_k, sel_k, raw_k):
        pl.semaphore_signal(barrier, inc=1, device_id={"kt": other}, device_id_type=MESH)
    for by in (1, slabs - 1):
        pl.semaphore_signal(
            barrier, inc=1, device_id={"slab": lax.rem(slab + by, slabs)}, device_id_type=MESH
        )
    pl.semaphore_wait(barrier, 5)

    def source(p):
        return prev.at[lax.rem(p, ne), p // ne]

    def y_copy(p):
        return pltpu.make_async_remote_copy(
            source(p), mate.at[p], y_send.at[p], y_recv.at[p],
            device_id={"kt": mate_k}, device_id_type=MESH,
        )

    def raw_copy(p):
        return pltpu.make_async_remote_copy(
            source(p), zraw.at[p], r_send.at[p], r_recv.at[p],
            device_id={"kt": raw_k}, device_id_type=MESH,
        )

    def sel_copy(p):
        return pltpu.make_async_remote_copy(
            own.at[p], zsel.at[p], s_send.at[p], s_recv.at[p],
            device_id={"kt": sel_k}, device_id_type=MESH,
        )

    units = 2 * (b // 128)

    def unit(i, part):
        part = part if i < units // 2 else 1 - part
        return 0, part, pl.ds((i % (units // 2)) * 128, 128)

    def y_unit(i, part):
        return pltpu.make_async_remote_copy(
            prev.at[0].at[unit(i, part)], mate.at[unit(i, part)], u_send.at[i], u_recv.at[i],
            device_id={"kt": mate_k}, device_id_type=MESH,
        )

    def sel_unit(i):
        return pltpu.make_async_remote_copy(
            own.at[unit(i, parity)], zsel.at[unit(i, parity)], v_send.at[i], v_recv.at[i],
            device_id={"kt": sel_k}, device_id_type=MESH,
        )

    def wait_sel(p):
        @pl.when(p == 0)
        def _():
            for i in range(units):
                sel_unit(i).wait_recv()

        @pl.when(p > 0)
        def _():
            sel_copy(p).wait_recv()

    def own_copy(p):
        return pltpu.make_async_copy(source(p), own.at[p], own_sem.at[p])

    def raw_half(p):
        return pltpu.make_async_remote_copy(
            stage.at[p], zraw.at[p, parity], r_send.at[p], r_recv.at[p],
            device_id={"kt": raw_k}, device_id_type=MESH,
        )

    def sel_half(p):
        return pltpu.make_async_remote_copy(
            stage.at[p], zsel.at[p, parity], s_send.at[p], s_recv.at[p],
            device_id={"kt": sel_k}, device_id_type=MESH,
        )

    def pass_sel(p, part):
        return pltpu.make_async_remote_copy(
            zsel.at[p, part], zraw.at[p, part], f_send.at[p], f_recv.at[p],
            device_id={"kt": mate_k}, device_id_type=MESH,
        )

    def pass_raw(p, part):
        return pltpu.make_async_remote_copy(
            zraw.at[p, part], zsel.at[p, part], f_send.at[p], f_recv.at[p],
            device_id={"kt": mate_k}, device_id_type=MESH,
        )

    def either(seam, half, whole):
        if not halve:
            whole()
            return
        pl.when(seam)(half)
        pl.when(jnp.logical_not(seam))(whole)

    def nothing():
        return None

    def pass_on(p):
        if not halve:
            return

        @pl.when(sel_got)
        def _():
            sel_half(p).wait_recv()
            pass_sel(p, parity).start()

        @pl.when(raw_got)
        def _():
            raw_half(p).wait_recv()
            pass_raw(p, parity).start()

    def arrived(p):
        either(sel_got, lambda: pass_raw(p, 1 - parity).wait_recv(), lambda: wait_sel(p))
        either(raw_got, lambda: pass_sel(p, 1 - parity).wait_recv(), lambda: raw_copy(p).wait_recv())

    def ret_copy(e):
        return pltpu.make_async_remote_copy(
            rhat.at[e, pl.ds(0, b)], bx.at[e], b_send.at[e], b_recv.at[e],
            device_id={"slab": jnp.maximum(slab - 1, 0)}, device_id_type=MESH,
        )

    def les_copy(e):
        return pltpu.make_async_remote_copy(
            les.at[e], bl.at[e], b_send.at[ne + e], b_recv.at[ne + e],
            device_id={"slab": jnp.maximum(slab - 1, 0)}, device_id_type=MESH,
        )

    def ret_store(e, part):
        return pltpu.make_async_copy(
            rhat.at[e, pl.ds(0, b), pl.ds(part * b, b)], ret_out.at[e, part], o_sem.at[e, part]
        )

    def les_store(e, part):
        return pltpu.make_async_copy(
            les.at[e, :, pl.ds(part * b, b)], les_out.at[e, part], o_sem.at[ne + e, part]
        )

    def begin(p):
        y_copy(p).start()
        own_copy(p).start()

    def begin_raw(p):
        either(raw_cut, nothing, lambda: raw_copy(p).start())

    for i in range(units):
        y_unit(i, 1 - parity).start()
    own_copy(0).start()
    begin_raw(0)
    for p in range(1, AHEAD):
        begin(p)

    def expand(ref):
        ref[b:, 0:b] = -ref[0:b, b:]
        ref[b:, b:] = ref[0:b, 0:b]

    chat[0:b, 0:b] = hop[0]
    chat[0:b, b:] = hop[1]
    expand(chat)

    @pl.when(slab == last)
    def _():
        for part in range(2):
            value = contact[part].astype(F32)
            flipped = value.T
            skew = value - flipped if part == 0 else value + flipped
            acc[:, part * b : (part + 1) * b] = skew
            for e in range(ne):
                bx[e, :, part * b : (part + 1) * b] = contact[part]
        for e in range(ne):
            for part in range(2):
                columns = slice(part * b, (part + 1) * b)
                bl[e, :, columns] = (-table[5 + e : 6 + e, :] * acc[:, columns]).astype(BF16)

    def phonon(p, part, rows):
        return (
            table[2:3, :] * zsel[p, part, rows].astype(F32)
            + table[3:4, :] * mate[p, part, rows].astype(F32)
            + table[4:5, :] * zraw[p, part, rows].astype(F32)
        )

    def over_rows(do):
        def one(i, carry):
            do(pl.ds(pl.multiple_of(i * rows_per, rows_per), rows_per))
            return carry

        lax.fori_loop(0, b // rows_per, one, 0)

    def mixed(chosen, p, part, rows):
        return (
            chosen * mate[p, part, rows].astype(F32) + (1.0 - chosen) * own[p, part, rows].astype(F32)
        ).astype(BF16)

    def half_choice():
        return jnp.where(raw_cut, 1.0 - table[1:2, :], table[0:1, :])

    def start_half(p):
        pl.when(raw_cut)(lambda: raw_half(p).start())
        pl.when(sel_cut)(lambda: sel_half(p).start())

    def meet_first():
        own_copy(0).wait()
        for i in range(units):
            y_unit(i, parity).wait_recv()
            _, part, rows = unit(i, parity)
            if halve and i < units // 2:

                @pl.when(jnp.logical_or(raw_cut, sel_cut))
                def _():
                    stage[0, rows] = mixed(half_choice(), 0, part, rows)
                    if i == units // 2 - 1:
                        start_half(0)

            def start_sel():
                own[0, part, rows] = mixed(table[0:1, :], 0, part, rows)
                sel_unit(i).start()

            either(sel_cut, nothing, start_sel)
        begin(AHEAD)

    def meet(p):
        y_copy(p).wait_recv()
        own_copy(p).wait()

        if halve:

            @pl.when(jnp.logical_or(raw_cut, sel_cut))
            def _():
                chosen = half_choice()

                def pick(rows):
                    stage[p, rows] = mixed(chosen, p, parity, rows)

                over_rows(pick)
                start_half(p)

        begin_raw(p)

        @pl.when(p + AHEAD < pieces)
        def _():
            begin(p + AHEAD)

    def prep(p):
        def pick(rows):
            for part in range(2):
                own[p, part, rows] = mixed(table[0:1, :], p, part, rows)

        def start_sel():
            over_rows(pick)
            sel_copy(p).start()

        either(sel_cut, nothing, start_sel)

    def congruence(left, boundary):
        wide[0:b, :] = boundary[...]
        expand(wide)
        for n, w in bands:
            mv[:, n : n + w] = dot(left[0:b, :], wide[:, n : n + w]).astype(BF16)
        return [(n, w, dot_nt(mv[...], left[n : n + w, :])) for n, w in bands]

    def ret_stage(e):
        @pl.when(slab < last)
        def _():
            ret_copy(e).wait_recv()

        for n, w, value in congruence(chat, bx.at[e]):
            acc[:, n : n + w] = value
        arrived(e)
        energy = energies[e]

        def make_system(rows):
            at = lax.broadcasted_iota(jnp.int32, (rows_per, b), 0) + rows.start
            eye = at == lax.broadcasted_iota(jnp.int32, (rows_per, b), 1)
            real = jnp.where(eye, energy - onsite[...], 0.0)
            imag = jnp.where(eye, broaden, 0.0)
            for part, diagonal in ((0, real), (1, imag)):
                columns = slice(part * b, (part + 1) * b)
                value = (
                    diagonal - ham[part, rows].astype(F32) - acc[rows, columns] - phonon(e, part, rows)
                )
                acc[rows, columns] = value
                sysb[rows, columns] = value.astype(BF16)

        over_rows(make_system)
        eye = lax.broadcasted_iota(jnp.int32, (128, 128), 0) == lax.broadcasted_iota(
            jnp.int32, (128, 128), 1
        )
        across, along = [], []
        for i in range(b // 128):
            rows = slice(i * 128, (i + 1) * 128)
            real = jnp.where(eye, acc[rows, i * 128 : (i + 1) * 128], 0.0)
            imag = jnp.where(eye, acc[rows, b + i * 128 : b + (i + 1) * 128], 0.0)
            for axis, found in ((0, across), (1, along)):
                re = jnp.sum(real, axis=axis, keepdims=True)
                im = jnp.sum(imag, axis=axis, keepdims=True)
                modulus = re * re + im * im
                found.append((re / modulus, -im / modulus))
        row_re = jnp.concatenate([found[0] for found in across], axis=1)
        row_im = jnp.concatenate([found[1] for found in across], axis=1)
        for i in range(b // 128):
            col_re, col_im = along[i]
            for half in range(2):
                start = i * 128 + half * 64
                rows = slice(start, start + 64)
                cre = col_re[half * 64 : half * 64 + 64]
                cim = col_im[half * 64 : half * 64 + 64]
                re, im = acc[rows, 0:b], acc[rows, b:]
                scaled_re = cre * re - cim * im
                scaled_im = cre * im + cim * re
                on = (
                    lax.broadcasted_iota(jnp.int32, (64, b), 0) + start
                    == lax.broadcasted_iota(jnp.int32, (64, b), 1)
                )
                first_re = jnp.where(on, 2.0 * row_re, 0.0) - (scaled_re * row_re - scaled_im * row_im)
                first_im = jnp.where(on, 2.0 * row_im, 0.0) - (scaled_re * row_im + scaled_im * row_re)
                first[rows, 0:b] = first_re
                first[rows, b:] = first_im
                fhat[rows, 0:b] = first_re.astype(BF16)
                fhat[rows, b:] = first_im.astype(BF16)
        expand(fhat)
        for n, w in bands:
            wide[0:b, n : n + w] = dot(sysb[...], fhat[:, n : n + w]).astype(BF16)
        expand(wide)
        for n, w in bands:
            rhat[e, 0:b, n : n + w] = (
                2.0 * first[:, n : n + w] - dot(fhat[0:b, :], wide[:, n : n + w])
            ).astype(BF16)

        @pl.when(slab > 0)
        def _():
            ret_copy(e).start()

        ret_store(e, 0).start()
        ret_store(e, 1).start()
        expand(rhat.at[e])
        for n, w in bands:
            ghat[e, 0:b, n : n + w] = dot(rhat[e, 0:b, :], chat[:, n : n + w]).astype(BF16)
        expand(ghat.at[e])

    def les_stage(e):
        p = ne + e

        def from_phonon():
            arrived(p)

            def make_source(rows):
                for part in range(2):
                    wide[rows, part * b : (part + 1) * b] = phonon(p, part, rows).astype(BF16)

            over_rows(make_source)
            expand(wide)
            for n, w in bands:
                mv[:, n : n + w] = dot(rhat[e, 0:b, :], wide[:, n : n + w]).astype(BF16)
            return [(n, w, dot_nt(mv[...], rhat[e, n : n + w, :])) for n, w in bands]

        def both(one, other):
            for n, w, value in one():
                acc[:, n : n + w] = value
            for n, w, value in other():
                les[e, :, n : n + w] = (acc[:, n : n + w] + value).astype(BF16)

        def from_boundary():
            return congruence(ghat.at[e], bl.at[e])

        def from_next_slab():
            les_copy(e).wait_recv()
            return from_boundary()

        pl.when(slab == last)(lambda: both(from_boundary, from_phonon))
        pl.when(slab < last)(lambda: both(from_phonon, from_next_slab))

        @pl.when(slab > 0)
        def _():
            les_copy(e).start()

        les_store(e, 0).start()
        les_store(e, 1).start()

    def turn(t, carry):
        @pl.when(jnp.logical_and(t >= 1, t < pieces))
        def _():
            prep(t)

        @pl.when(t + 1 < pieces)
        def _():
            meet(t + 1)

        c = t - LEAD

        @pl.when(jnp.logical_and(c + 1 >= 0, c + 1 < pieces))
        def _():
            pass_on(c + 1)

        @pl.when(jnp.logical_and(c >= 0, c < ne))
        def _():
            ret_stage(c)

        @pl.when(c >= ne)
        def _():
            les_stage(c - ne)

        return carry

    meet_first()
    lax.fori_loop(0, pieces + LEAD, turn, 0)

    for i in range(units):
        y_unit(i, 1 - parity).wait_send()
        either(sel_cut, nothing, lambda: sel_unit(i).wait_send())

    def drain(p, carry):
        @pl.when(p > 0)
        def _():
            y_copy(p).wait_send()
            either(sel_cut, nothing, lambda: sel_copy(p).wait_send())

        either(raw_cut, lambda: raw_half(p).wait_send(), lambda: raw_copy(p).wait_send())
        either(sel_cut, lambda: sel_half(p).wait_send(), nothing)
        either(sel_got, lambda: pass_sel(p, parity).wait_send(), nothing)
        either(raw_got, lambda: pass_raw(p, parity).wait_send(), nothing)
        return carry

    lax.fori_loop(0, pieces, drain, 0)

    def drain_out(e, carry):
        @pl.when(slab > 0)
        def _():
            ret_copy(e).wait_send()
            les_copy(e).wait_send()

        for part in range(2):
            ret_store(e, part).wait()
            les_store(e, part).wait()
        return carry

    lax.fori_loop(0, ne, drain_out, 0)


def body(
    energies, onsite, hamiltonian, hopping, contact, previous, neighbours, mode_index, mode_strength
):
    slabs, points = lax.axis_size("slab"), lax.axis_size("kt")
    ne, b = energies.shape[0], onsite.shape[-1]
    pieces = 2 * ne
    block = (pieces, 2, b, b)
    cat, square = (b, 2 * b), (2 * b, 2 * b)
    smem = pl.BlockSpec(memory_space=pltpu.SMEM)
    vmem = pl.BlockSpec(memory_space=pltpu.VMEM)
    anywhere = pl.BlockSpec(memory_space=pl.ANY)
    dma = pltpu.SemaphoreType.DMA
    table, plan = pl.pallas_call(
        functools.partial(agree, points, b),
        out_shape=(jax.ShapeDtypeStruct((16, b), F32), jax.ShapeDtypeStruct((1, 1), F32)),
        in_specs=[smem] * 4,
        out_specs=(vmem, smem),
        scratch_shapes=[
            pltpu.VMEM((8, 128), F32),
            pltpu.VMEM((points, 8, 128), F32),
            dma((points,)),
            dma((points,)),
        ],
        compiler_params=pltpu.CompilerParams(collective_id=0, has_side_effects=True),
        name="agree",
    )(energies, neighbours, mode_index, mode_strength)
    out = jax.ShapeDtypeStruct((ne, 2, b, b), BF16)

    def sweep(plan, *operands):
        halve = plan != WHOLE
        return pl.pallas_call(
            functools.partial(kernel, plan, slabs, points, ne, b),
            out_shape=(out, out),
            in_specs=[smem] + [vmem] * 5 + [anywhere],
            out_specs=(anywhere, anywhere),
            scratch_shapes=[
                pltpu.VMEM(block, BF16),
                pltpu.VMEM(block, BF16),
                pltpu.VMEM(block, BF16),
                pltpu.VMEM(block, BF16),
                pltpu.VMEM((pieces, b, b) if halve else (1, 16, 128), BF16),
                pltpu.VMEM((ne,) + cat, BF16),
                pltpu.VMEM((ne,) + cat, BF16),
                pltpu.VMEM(square, BF16),
                pltpu.VMEM((ne,) + square, BF16),
                pltpu.VMEM((ne,) + square, BF16),
                pltpu.VMEM((ne,) + cat, BF16),
                pltpu.VMEM(square, BF16),
                pltpu.VMEM(square, BF16),
                pltpu.VMEM(cat, BF16),
                pltpu.VMEM(cat, BF16),
                pltpu.VMEM(cat, F32),
                pltpu.VMEM(cat, F32),
            ]
            + [dma((pieces,))] * 11
            + [dma((pieces, 2))]
            + [dma((2 * (b // 128),))] * 4,
            compiler_params=pltpu.CompilerParams(
                collective_id=1 + plan,
                has_side_effects=True,
                vmem_limit_bytes=50 * 1024 * 1024,
            ),
            name=("sweep_whole", "sweep_seam", "sweep_down", "sweep_up")[plan],
        )(*operands)

    retarded, lesser = lax.switch(
        plan[0, 0].astype(jnp.int32),
        [functools.partial(sweep, which) for which in (WHOLE, SEAM, DOWN, UP)],
        energies, table, onsite[0], hamiltonian[0, 0], hopping[0, 0], contact[0],
        previous.reshape((ne, 2, 2, b, b)),
    )
    whole = (1, ne, 1, 2, b, b)
    return retarded.reshape(whole), lesser.reshape(whole)


def solution(mesh):
    in_specs = (
        P(),
        P("kt", "slab", None),
        P("kt", "slab", None, None, None),
        P("kt", "slab", None, None, None),
        P("kt", None, None, None),
        P("kt", None, "slab", None, None, None, None),
        P("kt", None),
        P("kt", None),
        P(),
    )
    out_specs = (P("kt", None, "slab", None, None, None), P("kt", None, "slab", None, None, None))
    return jax.shard_map(body, mesh=mesh, in_specs=in_specs, out_specs=out_specs, check_vma=False)
```

```python
import functools

import jax
import jax.numpy as jnp
from jax import lax
from jax.experimental import pallas as pl
from jax.experimental.pallas import tpu as pltpu
from jax.sharding import PartitionSpec as P

broaden = 0.05
fermi_level = 0.0
thermal = 0.1

MESH = pl.DeviceIdType.MESH
LEAD = 4
AHEAD = 2
F32 = jnp.float32
BF16 = jnp.bfloat16


def dot(a, b):
    return jnp.dot(a, b, preferred_element_type=F32)


def dot_nt(a, b):
    return lax.dot_general(a, b, (((1,), (1,)), ((), ())), preferred_element_type=F32)


def agree(
    points, b,
    energies, neighbours, mode_index, mode_strength,
    table, plan,
    mine, every, send, recv,
):
    k = lax.axis_index("kt")
    even = lax.rem(k, 2) == 0
    barrier = pltpu.get_barrier_semaphore()

    def peer(by):
        return {"kt": lax.rem(k + by, points)}

    def greet(by, carry):
        pl.semaphore_signal(barrier, inc=1, device_id=peer(by), device_id_type=MESH)
        return carry

    lax.fori_loop(1, points, greet, 0)
    pl.semaphore_wait(barrier, points - 1)
    left = jnp.where(neighbours[0, 0] == lax.rem(k - 1 + points, points), 1.0, 0.0)
    right = jnp.where(neighbours[0, 1] == lax.rem(k + 1, points), 1.0, 0.0)
    row = lax.broadcasted_iota(jnp.int32, (8, 128), 0)
    mine[...] = jnp.where(row == 0, left, right)
    every[k] = mine[...]

    def tell(by):
        return pltpu.make_async_remote_copy(
            mine, every.at[k], send.at[by], recv.at[k], device_id=peer(by), device_id_type=MESH
        )

    def hear(by):
        j = lax.rem(k + by, points)
        return pltpu.make_async_remote_copy(
            mine, every.at[j], send.at[by], recv.at[j], device_id=peer(by), device_id_type=MESH
        )

    def start(by, carry):
        tell(by).start()
        return carry

    def finish(by, carry):
        tell(by).wait_send()
        hear(by).wait_recv()
        return carry

    lax.fori_loop(1, points, start, 0)
    lax.fori_loop(1, points, finish, 0)

    def near(j):
        j = lax.rem(j + points, points)
        return every[j, 0:1, :], every[j, 1:2, :]

    left_2, right_2 = near(k + 2), near(k - 2)
    left_1, right_1 = near(k + 1), near(k - 1)
    chosen = jnp.where(even, left_2[0], right_2[1])
    wrapped = jnp.where(even, right_1[1], left_1[0])
    strength_left = mode_strength[mode_index[0, 0]]
    strength_right = mode_strength[mode_index[0, 1]]
    weight_sel = jnp.where(even, strength_left, strength_right)
    weight_other = jnp.where(even, strength_right, strength_left)
    other_near = jnp.where(even, right, left)
    full = jnp.zeros((1, 128), F32)
    rows = [
        chosen,
        wrapped,
        full + weight_sel,
        full + weight_other * other_near,
        full + weight_other * (1.0 - other_near),
    ]
    for e in range(energies.shape[0]):
        rows.append(1.0 / (1.0 + jnp.exp((full + energies[e] - fermi_level) / thermal)))
    for i, value in enumerate(rows):
        for start_at in range(0, b, 128):
            table[i : i + 1, start_at : start_at + 128] = value

    def pair_far(m):
        first, second = near(2 * m), near(2 * m + 1)
        return (1.0 - first[0]) * (1.0 - second[0]), (1.0 - first[1]) * (1.0 - second[1])

    def gather(m, found):
        up, down = pair_far(m)
        return jnp.maximum(found[0], up), jnp.maximum(found[1], down)

    up, down = lax.fori_loop(0, points // 2, gather, (full, full))
    seam = jnp.maximum(pair_far(0)[0], pair_far(points // 2 - 1)[1])
    plan[0, 0] = jnp.max(1.0 - seam + seam * (2.0 * (1.0 - down) + down * 3.0 * (1.0 - up)))


WHOLE, SEAM, DOWN, UP = range(4)


def kernel(
    plan, slabs, points, ne, b,
    energies, table, onsite, ham, hop, contact, prev,
    ret_out, les_out,
    own, mate, zsel, zraw, stage, bx, bl, chat, pair, les, wide, fhat, mv, sysb, acc, first,
    own_sem, y_send, y_recv, s_send, s_recv, r_send, r_recv, f_send, f_recv, b_send, b_recv, o_sem,
    u_send, u_recv, v_send, v_recv,
):
    slab = lax.axis_index("slab")
    k = lax.axis_index("kt")
    pieces = 2 * ne
    step = 2 - 4 * lax.rem(k, 2)
    parity = lax.rem(k, 2)
    mate_k = k + 1 - 2 * lax.rem(k, 2)
    sel_k = lax.rem(k + step + points, points)
    raw_k = lax.rem(k - step + points, points)
    halve = plan != WHOLE
    even = parity == 0
    odd = parity == 1
    if plan == SEAM:
        raw_cut = jnp.logical_or(k == 0, k == points - 1)
        sel_cut = jnp.logical_or(k == 1, k == points - 2)
        raw_got, sel_got = sel_cut, raw_cut
    elif plan == DOWN:
        raw_cut, sel_cut, raw_got, sel_got = even, odd, even, odd
    else:
        raw_cut, sel_cut, raw_got, sel_got = odd, even, odd, even
    last = slabs - 1
    bands = [(n, min(256, 2 * b - n)) for n in range(0, 2 * b, 256)]
    rows_per = 48

    barrier = pltpu.get_barrier_semaphore()
    for other in (mate_k, sel_k, raw_k):
        pl.semaphore_signal(barrier, inc=1, device_id={"kt": other}, device_id_type=MESH)
    for by in (1, slabs - 1):
        pl.semaphore_signal(
            barrier, inc=1, device_id={"slab": lax.rem(slab + by, slabs)}, device_id_type=MESH
        )
    pl.semaphore_wait(barrier, 5)

    def source(p):
        return prev.at[lax.rem(p, ne), p // ne]

    def y_copy(p):
        return pltpu.make_async_remote_copy(
            source(p), mate.at[p], y_send.at[p], y_recv.at[p],
            device_id={"kt": mate_k}, device_id_type=MESH,
        )

    def raw_copy(p):
        return pltpu.make_async_remote_copy(
            source(p), zraw.at[p], r_send.at[p], r_recv.at[p],
            device_id={"kt": raw_k}, device_id_type=MESH,
        )

    def sel_copy(p):
        return pltpu.make_async_remote_copy(
            own.at[p], zsel.at[p], s_send.at[p], s_recv.at[p],
            device_id={"kt": sel_k}, device_id_type=MESH,
        )

    per = 2 * (b // 128)
    units = AHEAD * per

    def unit(i, part):
        j = lax.rem(i, per)
        part = jnp.where(j < per // 2, part, 1 - part)
        return part, pl.ds(pl.multiple_of(lax.rem(j, per // 2) * 128, 128), 128)

    def y_unit(i, part):
        return pltpu.make_async_remote_copy(
            source(i // per).at[unit(i, part)], mate.at[i // per].at[unit(i, part)],
            u_send.at[i], u_recv.at[i], device_id={"kt": mate_k}, device_id_type=MESH,
        )

    def sel_unit(i):
        return pltpu.make_async_remote_copy(
            own.at[i // per].at[unit(i, parity)], zsel.at[i // per].at[unit(i, parity)],
            v_send.at[i], v_recv.at[i], device_id={"kt": sel_k}, device_id_type=MESH,
        )

    def wait_sel(p):
        @pl.when(p < AHEAD)
        def _():
            def one(j, carry):
                sel_unit(p * per + j).wait_recv()
                return carry

            lax.fori_loop(0, per, one, 0)

        @pl.when(p >= AHEAD)
        def _():
            sel_copy(p).wait_recv()

    def own_copy(p):
        return pltpu.make_async_copy(source(p), own.at[p], own_sem.at[p])

    def raw_half(p):
        return pltpu.make_async_remote_copy(
            stage.at[p], zraw.at[p, parity], r_send.at[p], r_recv.at[p],
            device_id={"kt": raw_k}, device_id_type=MESH,
        )

    def sel_half(p):
        return pltpu.make_async_remote_copy(
            stage.at[p], zsel.at[p, parity], s_send.at[p], s_recv.at[p],
            device_id={"kt": sel_k}, device_id_type=MESH,
        )

    def pass_sel(p, part):
        return pltpu.make_async_remote_copy(
            zsel.at[p, part], zraw.at[p, part], f_send.at[p], f_recv.at[p],
            device_id={"kt": mate_k}, device_id_type=MESH,
        )

    def pass_raw(p, part):
        return pltpu.make_async_remote_copy(
            zraw.at[p, part], zsel.at[p, part], f_send.at[p], f_recv.at[p],
            device_id={"kt": mate_k}, device_id_type=MESH,
        )

    def either(seam, half, whole):
        if not halve:
            whole()
            return
        pl.when(seam)(half)
        pl.when(jnp.logical_not(seam))(whole)

    def nothing():
        return None

    def pass_on(p):
        if not halve:
            return

        @pl.when(sel_got)
        def _():
            sel_half(p).wait_recv()
            pass_sel(p, parity).start()

        @pl.when(raw_got)
        def _():
            raw_half(p).wait_recv()
            pass_raw(p, parity).start()

    def arrived(p):
        either(sel_got, lambda: pass_raw(p, 1 - parity).wait_recv(), lambda: wait_sel(p))
        either(raw_got, lambda: pass_sel(p, 1 - parity).wait_recv(), lambda: raw_copy(p).wait_recv())

    def ret_copy(e):
        return pltpu.make_async_remote_copy(
            pair.at[e, 0, pl.ds(0, b)], bx.at[e], b_send.at[e], b_recv.at[e],
            device_id={"slab": jnp.maximum(slab - 1, 0)}, device_id_type=MESH,
        )

    def les_copy(e):
        return pltpu.make_async_remote_copy(
            les.at[e], bl.at[e], b_send.at[ne + e], b_recv.at[ne + e],
            device_id={"slab": jnp.maximum(slab - 1, 0)}, device_id_type=MESH,
        )

    def ret_store(e, part):
        return pltpu.make_async_copy(
            pair.at[e, 0, pl.ds(0, b), pl.ds(part * b, b)], ret_out.at[e, part], o_sem.at[e, part]
        )

    def les_store(e, part):
        return pltpu.make_async_copy(
            les.at[e, :, pl.ds(part * b, b)], les_out.at[e, part], o_sem.at[ne + e, part]
        )

    def begin(p):
        y_copy(p).start()
        own_copy(p).start()

    def begin_raw(p):
        either(raw_cut, nothing, lambda: raw_copy(p).start())

    def every_unit(do):
        def one(i, carry):
            do(i)
            return carry

        lax.fori_loop(0, units, one, 0)

    every_unit(lambda i: y_unit(i, 1 - parity).start())
    for p in range(AHEAD):
        own_copy(p).start()
    begin_raw(0)
    either(sel_cut, nothing, lambda: begin_raw(1))

    def expand(ref):
        ref[b:, 0:b] = -ref[0:b, b:]
        ref[b:, b:] = ref[0:b, 0:b]

    chat[0:b, 0:b] = hop[0]
    chat[0:b, b:] = hop[1]
    expand(chat)

    @pl.when(slab == last)
    def _():
        for part in range(2):
            value = contact[part].astype(F32)
            flipped = value.T
            skew = value - flipped if part == 0 else value + flipped
            acc[:, part * b : (part + 1) * b] = skew
            for e in range(ne):
                bx[e, :, part * b : (part + 1) * b] = contact[part]
        for e in range(ne):
            for part in range(2):
                columns = slice(part * b, (part + 1) * b)
                bl[e, :, columns] = (-table[5 + e : 6 + e, :] * acc[:, columns]).astype(BF16)

    def phonon(p, part, rows):
        return (
            table[2:3, :] * zsel[p, part, rows].astype(F32)
            + table[3:4, :] * mate[p, part, rows].astype(F32)
            + table[4:5, :] * zraw[p, part, rows].astype(F32)
        )

    def over_rows(do):
        def one(i, carry):
            do(pl.ds(pl.multiple_of(i * rows_per, rows_per), rows_per))
            return carry

        lax.fori_loop(0, b // rows_per, one, 0)

    def mixed(chosen, p, part, rows):
        return (
            chosen * mate[p, part, rows].astype(F32) + (1.0 - chosen) * own[p, part, rows].astype(F32)
        ).astype(BF16)

    def half_choice():
        return jnp.where(raw_cut, 1.0 - table[1:2, :], table[0:1, :])

    def start_half(p):
        pl.when(raw_cut)(lambda: raw_half(p).start())
        pl.when(sel_cut)(lambda: sel_half(p).start())

    def meet_unit(i, carry):
        p, j = i // per, lax.rem(i, per)

        @pl.when(j == 0)
        def _():
            own_copy(p).wait()

        y_unit(i, parity).wait_recv()
        part, rows = unit(i, parity)
        if halve:

            @pl.when(jnp.logical_and(jnp.logical_or(raw_cut, sel_cut), j < per // 2))
            def _():
                stage[p, rows] = mixed(half_choice(), p, part, rows)
                pl.when(j == per // 2 - 1)(lambda: start_half(p))

        def start_sel():
            own[p, part, rows] = mixed(table[0:1, :], p, part, rows)
            sel_unit(i).start()

        either(sel_cut, nothing, start_sel)

        @pl.when(j == per - 1)
        def _():
            begin(p + AHEAD)
            if halve:
                pl.when(jnp.logical_and(sel_cut, p + 1 < AHEAD))(lambda: begin_raw(p + 1))

        return carry

    def meet(p):
        y_copy(p).wait_recv()
        own_copy(p).wait()

        if halve:

            @pl.when(jnp.logical_or(raw_cut, sel_cut))
            def _():
                chosen = half_choice()

                def pick(rows):
                    stage[p, rows] = mixed(chosen, p, parity, rows)

                over_rows(pick)
                start_half(p)

        either(sel_cut, lambda: begin_raw(p), nothing)

        @pl.when(p + 1 < pieces)
        def _():
            either(sel_cut, nothing, lambda: begin_raw(p + 1))

        @pl.when(p + AHEAD < pieces)
        def _():
            begin(p + AHEAD)

    def prep(p):
        def pick(rows):
            for part in range(2):
                own[p, part, rows] = mixed(table[0:1, :], p, part, rows)

        def start_sel():
            over_rows(pick)
            sel_copy(p).start()

        either(sel_cut, nothing, start_sel)

    def self_energy(boundary):
        wide[0:b, :] = boundary[...]
        expand(wide)
        for n, w in bands:
            mv[:, n : n + w] = dot(chat[0:b, :], wide[:, n : n + w]).astype(BF16)
        for n, w in bands:
            acc[:, n : n + w] = dot_nt(mv[...], chat[n : n + w, :])

    def ret_stage(e):
        @pl.when(slab < last)
        def _():
            ret_copy(e).wait_recv()

        self_energy(bx.at[e])
        arrived(e)
        energy = energies[e]

        def make_system(rows):
            at = lax.broadcasted_iota(jnp.int32, (rows_per, b), 0) + rows.start
            eye = at == lax.broadcasted_iota(jnp.int32, (rows_per, b), 1)
            real = jnp.where(eye, energy - onsite[...], 0.0)
            imag = jnp.where(eye, broaden, 0.0)
            for part, diagonal in ((0, real), (1, imag)):
                columns = slice(part * b, (part + 1) * b)
                value = (
                    diagonal - ham[part, rows].astype(F32) - acc[rows, columns] - phonon(e, part, rows)
                )
                acc[rows, columns] = value
                sysb[rows, columns] = value.astype(BF16)

        over_rows(make_system)
        eye = lax.broadcasted_iota(jnp.int32, (128, 128), 0) == lax.broadcasted_iota(
            jnp.int32, (128, 128), 1
        )
        across, along = [], []
        for i in range(b // 128):
            rows = slice(i * 128, (i + 1) * 128)
            real = jnp.where(eye, acc[rows, i * 128 : (i + 1) * 128], 0.0)
            imag = jnp.where(eye, acc[rows, b + i * 128 : b + (i + 1) * 128], 0.0)
            for axis, found in ((0, across), (1, along)):
                re = jnp.sum(real, axis=axis, keepdims=True)
                im = jnp.sum(imag, axis=axis, keepdims=True)
                modulus = re * re + im * im
                found.append((re / modulus, -im / modulus))
        row_re = jnp.concatenate([found[0] for found in across], axis=1)
        row_im = jnp.concatenate([found[1] for found in across], axis=1)
        for i in range(b // 128):
            col_re, col_im = along[i]
            for half in range(2):
                start = i * 128 + half * 64
                rows = slice(start, start + 64)
                cre = col_re[half * 64 : half * 64 + 64]
                cim = col_im[half * 64 : half * 64 + 64]
                re, im = acc[rows, 0:b], acc[rows, b:]
                scaled_re = cre * re - cim * im
                scaled_im = cre * im + cim * re
                on = (
                    lax.broadcasted_iota(jnp.int32, (64, b), 0) + start
                    == lax.broadcasted_iota(jnp.int32, (64, b), 1)
                )
                first_re = jnp.where(on, 2.0 * row_re, 0.0) - (scaled_re * row_re - scaled_im * row_im)
                first_im = jnp.where(on, 2.0 * row_im, 0.0) - (scaled_re * row_im + scaled_im * row_re)
                first[rows, 0:b] = first_re
                first[rows, b:] = first_im
                fhat[rows, 0:b] = first_re.astype(BF16)
                fhat[rows, b:] = first_im.astype(BF16)
        expand(fhat)
        for n, w in bands:
            wide[0:b, n : n + w] = dot(sysb[...], fhat[:, n : n + w]).astype(BF16)
        expand(wide)
        for n, w in bands:
            pair[e, 0, 0:b, n : n + w] = (
                2.0 * first[:, n : n + w] - dot(fhat[0:b, :], wide[:, n : n + w])
            ).astype(BF16)

        @pl.when(slab > 0)
        def _():
            ret_copy(e).start()

        ret_store(e, 0).start()
        ret_store(e, 1).start()
        expand(pair.at[e, 0])
        for n, w in bands:
            pair[e, 1, 0:b, n : n + w] = dot(pair[e, 0, 0:b, :], chat[:, n : n + w]).astype(BF16)
        expand(pair.at[e, 1])

    def les_stage(e):
        p = ne + e
        acc[...] = jnp.zeros_like(acc)

        def term(i, carry):
            which = jnp.where(slab == last, 1 - i, i)

            @pl.when(which == 0)
            def _():
                arrived(p)

                def make_source(rows):
                    for part in range(2):
                        wide[rows, part * b : (part + 1) * b] = phonon(p, part, rows).astype(BF16)

                over_rows(make_source)

            @pl.when(which == 1)
            def _():
                pl.when(slab < last)(lambda: les_copy(e).wait_recv())
                wide[0:b, :] = bl[e]

            expand(wide)
            for n, w in bands:
                mv[:, n : n + w] = dot(pair[e, which, 0:b, :], wide[:, n : n + w]).astype(BF16)
            for n, w in bands:
                acc[:, n : n + w] += dot_nt(mv[...], pair[e, which, n : n + w, :])
            return carry

        lax.fori_loop(0, 2, term, 0)
        les[e] = acc[...].astype(BF16)

        @pl.when(slab > 0)
        def _():
            les_copy(e).start()

        les_store(e, 0).start()
        les_store(e, 1).start()

    def turn(t, carry):
        @pl.when(jnp.logical_and(t >= AHEAD, t < pieces))
        def _():
            prep(t)

        @pl.when(jnp.logical_and(t + 1 >= AHEAD, t + 1 < pieces))
        def _():
            meet(t + 1)

        c = t - LEAD

        @pl.when(jnp.logical_and(c + 1 >= 0, c + 1 < pieces))
        def _():
            pass_on(c + 1)

        @pl.when(jnp.logical_and(c >= 0, c < ne))
        def _():
            ret_stage(c)

        @pl.when(c >= ne)
        def _():
            les_stage(c - ne)

        return carry

    lax.fori_loop(0, units, meet_unit, 0)
    either(sel_cut, nothing, lambda: begin_raw(AHEAD))
    lax.fori_loop(0, pieces + LEAD, turn, 0)

    every_unit(lambda i: y_unit(i, 1 - parity).wait_send())
    either(sel_cut, nothing, lambda: every_unit(lambda i: sel_unit(i).wait_send()))

    def drain(p, carry):
        @pl.when(p >= AHEAD)
        def _():
            y_copy(p).wait_send()
            either(sel_cut, nothing, lambda: sel_copy(p).wait_send())

        either(raw_cut, lambda: raw_half(p).wait_send(), lambda: raw_copy(p).wait_send())
        either(sel_cut, lambda: sel_half(p).wait_send(), nothing)
        either(sel_got, lambda: pass_sel(p, parity).wait_send(), nothing)
        either(raw_got, lambda: pass_raw(p, parity).wait_send(), nothing)
        return carry

    lax.fori_loop(0, pieces, drain, 0)

    def drain_out(e, carry):
        @pl.when(slab > 0)
        def _():
            ret_copy(e).wait_send()
            les_copy(e).wait_send()

        for part in range(2):
            ret_store(e, part).wait()
            les_store(e, part).wait()
        return carry

    lax.fori_loop(0, ne, drain_out, 0)


def body(
    energies, onsite, hamiltonian, hopping, contact, previous, neighbours, mode_index, mode_strength
):
    slabs, points = lax.axis_size("slab"), lax.axis_size("kt")
    ne, b = energies.shape[0], onsite.shape[-1]
    pieces = 2 * ne
    block = (pieces, 2, b, b)
    cat, square = (b, 2 * b), (2 * b, 2 * b)
    smem = pl.BlockSpec(memory_space=pltpu.SMEM)
    vmem = pl.BlockSpec(memory_space=pltpu.VMEM)
    anywhere = pl.BlockSpec(memory_space=pl.ANY)
    dma = pltpu.SemaphoreType.DMA
    table, plan = pl.pallas_call(
        functools.partial(agree, points, b),
        out_shape=(jax.ShapeDtypeStruct((16, b), F32), jax.ShapeDtypeStruct((1, 1), F32)),
        in_specs=[smem] * 4,
        out_specs=(vmem, smem),
        scratch_shapes=[
            pltpu.VMEM((8, 128), F32),
            pltpu.VMEM((points, 8, 128), F32),
            dma((points,)),
            dma((points,)),
        ],
        compiler_params=pltpu.CompilerParams(collective_id=0, has_side_effects=True),
        name="agree",
    )(energies, neighbours, mode_index, mode_strength)
    out = jax.ShapeDtypeStruct((ne, 2, b, b), BF16)

    def sweep(plan, *operands):
        halve = plan != WHOLE
        return pl.pallas_call(
            functools.partial(kernel, plan, slabs, points, ne, b),
            out_shape=(out, out),
            in_specs=[smem] + [vmem] * 5 + [anywhere],
            out_specs=(anywhere, anywhere),
            scratch_shapes=[
                pltpu.VMEM(block, BF16),
                pltpu.VMEM(block, BF16),
                pltpu.VMEM(block, BF16),
                pltpu.VMEM(block, BF16),
                pltpu.VMEM((pieces, b, b) if halve else (1, 16, 128), BF16),
                pltpu.VMEM((ne,) + cat, BF16),
                pltpu.VMEM((ne,) + cat, BF16),
                pltpu.VMEM(square, BF16),
                pltpu.VMEM((ne, 2) + square, BF16),
                pltpu.VMEM((ne,) + cat, BF16),
                pltpu.VMEM(square, BF16),
                pltpu.VMEM(square, BF16),
                pltpu.VMEM(cat, BF16),
                pltpu.VMEM(cat, BF16),
                pltpu.VMEM(cat, F32),
                pltpu.VMEM(cat, F32),
            ]
            + [dma((pieces,))] * 11
            + [dma((pieces, 2))]
            + [dma((AHEAD * 2 * (b // 128),))] * 4,
            compiler_params=pltpu.CompilerParams(
                collective_id=1 + plan,
                has_side_effects=True,
                vmem_limit_bytes=50 * 1024 * 1024,
            ),
            name=("sweep_whole", "sweep_seam", "sweep_down", "sweep_up")[plan],
        )(*operands)

    retarded, lesser = lax.switch(
        plan[0, 0].astype(jnp.int32),
        [functools.partial(sweep, which) for which in (WHOLE, SEAM, DOWN, UP)],
        energies, table, onsite[0], hamiltonian[0, 0], hopping[0, 0], contact[0],
        previous.reshape((ne, 2, 2, b, b)),
    )
    whole = (1, ne, 1, 2, b, b)
    return retarded.reshape(whole), lesser.reshape(whole)


def solution(mesh):
    in_specs = (
        P(),
        P("kt", "slab", None),
        P("kt", "slab", None, None, None),
        P("kt", "slab", None, None, None),
        P("kt", None, None, None),
        P("kt", None, "slab", None, None, None, None),
        P("kt", None),
        P("kt", None),
        P(),
    )
    out_specs = (P("kt", None, "slab", None, None, None), P("kt", None, "slab", None, None, None))
    return jax.shard_map(body, mesh=mesh, in_specs=in_specs, out_specs=out_specs, check_vma=False)
```

```python
import functools

import jax
import jax.numpy as jnp
from jax import lax
from jax.experimental import pallas as pl
from jax.experimental.pallas import tpu as pltpu
from jax.sharding import PartitionSpec as P

broaden = 0.05
fermi_level = 0.0
thermal = 0.1

MESH = pl.DeviceIdType.MESH
LEAD = 4
AHEAD = 2
F32 = jnp.float32
BF16 = jnp.bfloat16


def dot(a, b):
    return jnp.dot(a, b, preferred_element_type=F32)


def dot_nt(a, b):
    return lax.dot_general(a, b, (((1,), (1,)), ((), ())), preferred_element_type=F32)


def agree(
    points, b,
    energies, neighbours, mode_index, mode_strength,
    table, plan,
    mine, every, send, recv,
):
    k = lax.axis_index("kt")
    even = lax.rem(k, 2) == 0
    barrier = pltpu.get_barrier_semaphore()

    def peer(by):
        return {"kt": lax.rem(k + by, points)}

    def greet(by, carry):
        pl.semaphore_signal(barrier, inc=1, device_id=peer(by), device_id_type=MESH)
        return carry

    lax.fori_loop(1, points, greet, 0)
    pl.semaphore_wait(barrier, points - 1)
    left = jnp.where(neighbours[0, 0] == lax.rem(k - 1 + points, points), 1.0, 0.0)
    right = jnp.where(neighbours[0, 1] == lax.rem(k + 1, points), 1.0, 0.0)
    row = lax.broadcasted_iota(jnp.int32, (8, 128), 0)
    mine[...] = jnp.where(row == 0, left, right)
    every[k] = mine[...]

    def tell(by):
        return pltpu.make_async_remote_copy(
            mine, every.at[k], send.at[by], recv.at[k], device_id=peer(by), device_id_type=MESH
        )

    def hear(by):
        j = lax.rem(k + by, points)
        return pltpu.make_async_remote_copy(
            mine, every.at[j], send.at[by], recv.at[j], device_id=peer(by), device_id_type=MESH
        )

    def start(by, carry):
        tell(by).start()
        return carry

    def finish(by, carry):
        tell(by).wait_send()
        hear(by).wait_recv()
        return carry

    lax.fori_loop(1, points, start, 0)
    lax.fori_loop(1, points, finish, 0)

    def near(j):
        j = lax.rem(j + points, points)
        return every[j, 0:1, :], every[j, 1:2, :]

    left_2, right_2 = near(k + 2), near(k - 2)
    left_1, right_1 = near(k + 1), near(k - 1)
    chosen = jnp.where(even, left_2[0], right_2[1])
    wrapped = jnp.where(even, right_1[1], left_1[0])
    strength_left = mode_strength[mode_index[0, 0]]
    strength_right = mode_strength[mode_index[0, 1]]
    weight_sel = jnp.where(even, strength_left, strength_right)
    weight_other = jnp.where(even, strength_right, strength_left)
    other_near = jnp.where(even, right, left)
    full = jnp.zeros((1, 128), F32)
    rows = [
        chosen,
        wrapped,
        full + weight_sel,
        full + weight_other * other_near,
        full + weight_other * (1.0 - other_near),
    ]
    for e in range(energies.shape[0]):
        rows.append(1.0 / (1.0 + jnp.exp((full + energies[e] - fermi_level) / thermal)))
    for i, value in enumerate(rows):
        for start_at in range(0, b, 128):
            table[i : i + 1, start_at : start_at + 128] = value

    def pair_far(m):
        first, second = near(2 * m), near(2 * m + 1)
        return (1.0 - first[0]) * (1.0 - second[0]), (1.0 - first[1]) * (1.0 - second[1])

    def gather(m, found):
        up, down = pair_far(m)
        return jnp.maximum(found[0], up), jnp.maximum(found[1], down)

    up, down = lax.fori_loop(0, points // 2, gather, (full, full))
    seam = jnp.maximum(pair_far(0)[0], pair_far(points // 2 - 1)[1])
    plan[0, 0] = jnp.max(1.0 - seam + seam * (2.0 * (1.0 - down) + down * 3.0 * (1.0 - up)))


WHOLE, SEAM, DOWN, UP = range(4)


def kernel(
    plan, slabs, points, ne, b,
    energies, table, onsite, ham, hop, contact, prev,
    ret_out, les_out,
    own, mate, zsel, zraw, stage, bx, bl, chat, pair, les, wide, fhat, mv, sysb, acc, first,
    own_sem, y_send, y_recv, s_send, s_recv, r_send, r_recv, f_send, f_recv, b_send, b_recv, o_sem,
    u_send, u_recv, v_send, v_recv,
):
    slab = lax.axis_index("slab")
    k = lax.axis_index("kt")
    pieces = 2 * ne
    step = 2 - 4 * lax.rem(k, 2)
    parity = lax.rem(k, 2)
    mate_k = k + 1 - 2 * lax.rem(k, 2)
    sel_k = lax.rem(k + step + points, points)
    raw_k = lax.rem(k - step + points, points)
    halve = plan != WHOLE
    even = parity == 0
    odd = parity == 1
    if plan == SEAM:
        raw_cut = jnp.logical_or(k == 0, k == points - 1)
        sel_cut = jnp.logical_or(k == 1, k == points - 2)
        raw_got, sel_got = sel_cut, raw_cut
    elif plan == DOWN:
        raw_cut, sel_cut, raw_got, sel_got = even, odd, even, odd
    else:
        raw_cut, sel_cut, raw_got, sel_got = odd, even, odd, even
    last = slabs - 1
    bands = [(n, min(256, 2 * b - n)) for n in range(0, 2 * b, 256)]
    rows_per = 48

    barrier = pltpu.get_barrier_semaphore()
    for other in (mate_k, sel_k, raw_k):
        pl.semaphore_signal(barrier, inc=1, device_id={"kt": other}, device_id_type=MESH)
    for by in (1, slabs - 1):
        pl.semaphore_signal(
            barrier, inc=1, device_id={"slab": lax.rem(slab + by, slabs)}, device_id_type=MESH
        )
    pl.semaphore_wait(barrier, 5)

    def source(p):
        return prev.at[lax.rem(p, ne), p // ne]

    def y_copy(p):
        return pltpu.make_async_remote_copy(
            source(p), mate.at[p], y_send.at[p], y_recv.at[p],
            device_id={"kt": mate_k}, device_id_type=MESH,
        )

    def raw_copy(p):
        return pltpu.make_async_remote_copy(
            source(p), zraw.at[p], r_send.at[p], r_recv.at[p],
            device_id={"kt": raw_k}, device_id_type=MESH,
        )

    def sel_copy(p):
        return pltpu.make_async_remote_copy(
            own.at[p], zsel.at[p], s_send.at[p], s_recv.at[p],
            device_id={"kt": sel_k}, device_id_type=MESH,
        )

    per = 2 * (b // 128)
    units = AHEAD * per

    def unit(i, part):
        j = lax.rem(i, per)
        part = jnp.where(j < per // 2, part, 1 - part)
        return part, pl.ds(pl.multiple_of(lax.rem(j, per // 2) * 128, 128), 128)

    def y_unit(i, part):
        return pltpu.make_async_remote_copy(
            source(i // per).at[unit(i, part)], mate.at[i // per].at[unit(i, part)],
            u_send.at[i], u_recv.at[i], device_id={"kt": mate_k}, device_id_type=MESH,
        )

    def sel_unit(i):
        return pltpu.make_async_remote_copy(
            own.at[i // per].at[unit(i, parity)], zsel.at[i // per].at[unit(i, parity)],
            v_send.at[i], v_recv.at[i], device_id={"kt": sel_k}, device_id_type=MESH,
        )

    def wait_sel(p):
        @pl.when(p < AHEAD)
        def _():
            def one(j, carry):
                sel_unit(p * per + j).wait_recv()
                return carry

            lax.fori_loop(0, per, one, 0)

        @pl.when(p >= AHEAD)
        def _():
            sel_copy(p).wait_recv()

    def own_copy(p):
        return pltpu.make_async_copy(source(p), own.at[p], own_sem.at[p])

    def raw_half(p):
        return pltpu.make_async_remote_copy(
            stage.at[p], zraw.at[p, parity], r_send.at[p], r_recv.at[p],
            device_id={"kt": raw_k}, device_id_type=MESH,
        )

    def sel_half(p):
        return pltpu.make_async_remote_copy(
            stage.at[p], zsel.at[p, parity], s_send.at[p], s_recv.at[p],
            device_id={"kt": sel_k}, device_id_type=MESH,
        )

    def pass_sel(p, part):
        return pltpu.make_async_remote_copy(
            zsel.at[p, part], zraw.at[p, part], f_send.at[p], f_recv.at[p],
            device_id={"kt": mate_k}, device_id_type=MESH,
        )

    def pass_raw(p, part):
        return pltpu.make_async_remote_copy(
            zraw.at[p, part], zsel.at[p, part], f_send.at[p], f_recv.at[p],
            device_id={"kt": mate_k}, device_id_type=MESH,
        )

    def either(seam, half, whole):
        if not halve:
            whole()
            return
        pl.when(seam)(half)
        pl.when(jnp.logical_not(seam))(whole)

    def nothing():
        return None

    def pass_on(p):
        if not halve:
            return

        @pl.when(sel_got)
        def _():
            sel_half(p).wait_recv()
            pass_sel(p, parity).start()

        @pl.when(raw_got)
        def _():
            raw_half(p).wait_recv()
            pass_raw(p, parity).start()

    def arrived(p):
        either(sel_got, lambda: pass_raw(p, 1 - parity).wait_recv(), lambda: wait_sel(p))
        either(raw_got, lambda: pass_sel(p, 1 - parity).wait_recv(), lambda: raw_copy(p).wait_recv())

    def ret_copy(e):
        return pltpu.make_async_remote_copy(
            pair.at[e, 0, pl.ds(0, b)], bx.at[e], b_send.at[e], b_recv.at[e],
            device_id={"slab": jnp.maximum(slab - 1, 0)}, device_id_type=MESH,
        )

    def les_copy(e):
        return pltpu.make_async_remote_copy(
            les.at[e], bl.at[e], b_send.at[ne + e], b_recv.at[ne + e],
            device_id={"slab": jnp.maximum(slab - 1, 0)}, device_id_type=MESH,
        )

    def ret_store(e, part):
        return pltpu.make_async_copy(
            pair.at[e, 0, pl.ds(0, b), pl.ds(part * b, b)], ret_out.at[e, part], o_sem.at[e, part]
        )

    def les_store(e, part):
        return pltpu.make_async_copy(
            les.at[e, :, pl.ds(part * b, b)], les_out.at[e, part], o_sem.at[ne + e, part]
        )

    def begin(p):
        y_copy(p).start()
        own_copy(p).start()

    def begin_raw(p):
        either(raw_cut, nothing, lambda: raw_copy(p).start())

    def every_unit(do):
        def one(i, carry):
            do(i)
            return carry

        lax.fori_loop(0, units, one, 0)

    every_unit(lambda i: y_unit(i, 1 - parity).start())
    for p in range(AHEAD):
        own_copy(p).start()
    begin_raw(0)
    either(sel_cut, nothing, lambda: begin_raw(1))

    def expand(ref):
        ref[b:, 0:b] = -ref[0:b, b:]
        ref[b:, b:] = ref[0:b, 0:b]

    chat[0:b, 0:b] = hop[0]
    chat[0:b, b:] = hop[1]
    expand(chat)

    @pl.when(slab == last)
    def _():
        for part in range(2):
            value = contact[part].astype(F32)
            flipped = value.T
            skew = value - flipped if part == 0 else value + flipped
            acc[:, part * b : (part + 1) * b] = skew
            for e in range(ne):
                bx[e, :, part * b : (part + 1) * b] = contact[part]
        for e in range(ne):
            for part in range(2):
                columns = slice(part * b, (part + 1) * b)
                bl[e, :, columns] = (-table[5 + e : 6 + e, :] * acc[:, columns]).astype(BF16)

    def phonon(p, part, rows):
        return (
            table[2:3, :] * zsel[p, part, rows].astype(F32)
            + table[3:4, :] * mate[p, part, rows].astype(F32)
            + table[4:5, :] * zraw[p, part, rows].astype(F32)
        )

    def over_rows(do, unroll=False):
        def one(i, carry):
            do(pl.ds(pl.multiple_of(i * rows_per, rows_per), rows_per))
            return carry

        lax.fori_loop(0, b // rows_per, one, 0, unroll=unroll)

    def mixed(chosen, p, part, rows):
        return (
            chosen * mate[p, part, rows].astype(F32) + (1.0 - chosen) * own[p, part, rows].astype(F32)
        ).astype(BF16)

    def half_choice():
        return jnp.where(raw_cut, 1.0 - table[1:2, :], table[0:1, :])

    def start_half(p):
        pl.when(raw_cut)(lambda: raw_half(p).start())
        pl.when(sel_cut)(lambda: sel_half(p).start())

    def meet_unit(i, carry):
        p, j = i // per, lax.rem(i, per)

        @pl.when(j == 0)
        def _():
            own_copy(p).wait()

        y_unit(i, parity).wait_recv()
        part, rows = unit(i, parity)
        if halve:

            @pl.when(jnp.logical_and(jnp.logical_or(raw_cut, sel_cut), j < per // 2))
            def _():
                stage[p, rows] = mixed(half_choice(), p, part, rows)
                pl.when(j == per // 2 - 1)(lambda: start_half(p))

        def start_sel():
            own[p, part, rows] = mixed(table[0:1, :], p, part, rows)
            sel_unit(i).start()

        either(sel_cut, nothing, start_sel)

        @pl.when(j == per - 1)
        def _():
            begin(p + AHEAD)
            if halve:
                pl.when(jnp.logical_and(sel_cut, p + 1 < AHEAD))(lambda: begin_raw(p + 1))

        return carry

    def meet(p):
        y_copy(p).wait_recv()
        own_copy(p).wait()

        if halve:

            @pl.when(jnp.logical_or(raw_cut, sel_cut))
            def _():
                chosen = half_choice()

                def pick(rows):
                    stage[p, rows] = mixed(chosen, p, parity, rows)

                over_rows(pick)
                start_half(p)

        either(sel_cut, lambda: begin_raw(p), nothing)

        @pl.when(p + 1 < pieces)
        def _():
            either(sel_cut, nothing, lambda: begin_raw(p + 1))

        @pl.when(p + AHEAD < pieces)
        def _():
            begin(p + AHEAD)

    def prep(p):
        def pick(rows):
            for part in range(2):
                own[p, part, rows] = mixed(table[0:1, :], p, part, rows)

        def start_sel():
            over_rows(pick)
            sel_copy(p).start()

        either(sel_cut, nothing, start_sel)

    def self_energy(boundary):
        wide[0:b, :] = boundary[...]
        expand(wide)
        for n, w in bands:
            mv[:, n : n + w] = dot(chat[0:b, :], wide[:, n : n + w]).astype(BF16)
        for n, w in bands:
            acc[:, n : n + w] = dot_nt(mv[...], chat[n : n + w, :])

    def ret_stage(e):
        @pl.when(slab < last)
        def _():
            ret_copy(e).wait_recv()

        self_energy(bx.at[e])
        arrived(e)
        energy = energies[e]

        def make_system(rows):
            at = lax.broadcasted_iota(jnp.int32, (rows_per, b), 0) + rows.start
            eye = at == lax.broadcasted_iota(jnp.int32, (rows_per, b), 1)
            real = jnp.where(eye, energy - onsite[...], 0.0)
            imag = jnp.where(eye, broaden, 0.0)
            for part, diagonal in ((0, real), (1, imag)):
                columns = slice(part * b, (part + 1) * b)
                value = (
                    diagonal - ham[part, rows].astype(F32) - acc[rows, columns] - phonon(e, part, rows)
                )
                acc[rows, columns] = value
                sysb[rows, columns] = value.astype(BF16)

        over_rows(make_system)
        eye = lax.broadcasted_iota(jnp.int32, (128, 128), 0) == lax.broadcasted_iota(
            jnp.int32, (128, 128), 1
        )
        across, along = [], []
        for i in range(b // 128):
            rows = slice(i * 128, (i + 1) * 128)
            real = jnp.where(eye, acc[rows, i * 128 : (i + 1) * 128], 0.0)
            imag = jnp.where(eye, acc[rows, b + i * 128 : b + (i + 1) * 128], 0.0)
            for axis, found in ((0, across), (1, along)):
                re = jnp.sum(real, axis=axis, keepdims=True)
                im = jnp.sum(imag, axis=axis, keepdims=True)
                modulus = re * re + im * im
                found.append((re / modulus, -im / modulus))
        row_re = jnp.concatenate([found[0] for found in across], axis=1)
        row_im = jnp.concatenate([found[1] for found in across], axis=1)
        for i in range(b // 128):
            col_re, col_im = along[i]
            for half in range(2):
                start = i * 128 + half * 64
                rows = slice(start, start + 64)
                cre = col_re[half * 64 : half * 64 + 64]
                cim = col_im[half * 64 : half * 64 + 64]
                re, im = acc[rows, 0:b], acc[rows, b:]
                scaled_re = cre * re - cim * im
                scaled_im = cre * im + cim * re
                on = (
                    lax.broadcasted_iota(jnp.int32, (64, b), 0) + start
                    == lax.broadcasted_iota(jnp.int32, (64, b), 1)
                )
                first_re = jnp.where(on, 2.0 * row_re, 0.0) - (scaled_re * row_re - scaled_im * row_im)
                first_im = jnp.where(on, 2.0 * row_im, 0.0) - (scaled_re * row_im + scaled_im * row_re)
                first[rows, 0:b] = first_re
                first[rows, b:] = first_im
                fhat[rows, 0:b] = first_re.astype(BF16)
                fhat[rows, b:] = first_im.astype(BF16)
        expand(fhat)
        for n, w in bands:
            wide[0:b, n : n + w] = dot(sysb[...], fhat[:, n : n + w]).astype(BF16)
        expand(wide)
        for n, w in bands:
            pair[e, 0, 0:b, n : n + w] = (
                2.0 * first[:, n : n + w] - dot(fhat[0:b, :], wide[:, n : n + w])
            ).astype(BF16)

        @pl.when(slab > 0)
        def _():
            ret_copy(e).start()

        ret_store(e, 0).start()
        ret_store(e, 1).start()
        expand(pair.at[e, 0])
        for n, w in bands:
            pair[e, 1, 0:b, n : n + w] = dot(pair[e, 0, 0:b, :], chat[:, n : n + w]).astype(BF16)
        expand(pair.at[e, 1])

    def les_stage(e):
        p = ne + e
        acc[...] = jnp.zeros_like(acc)

        def term(i, carry):
            which = jnp.where(slab == last, 1 - i, i)

            @pl.when(which == 0)
            def _():
                arrived(p)

                def make_source(rows):
                    for part in range(2):
                        wide[rows, part * b : (part + 1) * b] = phonon(p, part, rows).astype(BF16)

                over_rows(make_source, True)

            @pl.when(which == 1)
            def _():
                pl.when(slab < last)(lambda: les_copy(e).wait_recv())
                wide[0:b, :] = bl[e]

            expand(wide)
            for n, w in bands:
                mv[:, n : n + w] = dot(pair[e, which, 0:b, :], wide[:, n : n + w]).astype(BF16)
            for n, w in bands:
                acc[:, n : n + w] += dot_nt(mv[...], pair[e, which, n : n + w, :])
            return carry

        lax.fori_loop(0, 2, term, 0)
        les[e] = acc[...].astype(BF16)

        @pl.when(slab > 0)
        def _():
            les_copy(e).start()

        les_store(e, 0).start()
        les_store(e, 1).start()

    def turn(t, carry):
        @pl.when(jnp.logical_and(t >= AHEAD, t < pieces))
        def _():
            prep(t)

        @pl.when(jnp.logical_and(t + 1 >= AHEAD, t + 1 < pieces))
        def _():
            meet(t + 1)

        c = t - LEAD

        @pl.when(jnp.logical_and(c + 1 >= 0, c + 1 < pieces))
        def _():
            pass_on(c + 1)

        @pl.when(jnp.logical_and(c >= 0, c < ne))
        def _():
            ret_stage(c)

        @pl.when(c >= ne)
        def _():
            les_stage(c - ne)

        return carry

    lax.fori_loop(0, units, meet_unit, 0)
    either(sel_cut, nothing, lambda: begin_raw(AHEAD))
    lax.fori_loop(0, pieces + LEAD, turn, 0)

    every_unit(lambda i: y_unit(i, 1 - parity).wait_send())
    either(sel_cut, nothing, lambda: every_unit(lambda i: sel_unit(i).wait_send()))

    def drain(p, carry):
        @pl.when(p >= AHEAD)
        def _():
            y_copy(p).wait_send()
            either(sel_cut, nothing, lambda: sel_copy(p).wait_send())

        either(raw_cut, lambda: raw_half(p).wait_send(), lambda: raw_copy(p).wait_send())
        either(sel_cut, lambda: sel_half(p).wait_send(), nothing)
        either(sel_got, lambda: pass_sel(p, parity).wait_send(), nothing)
        either(raw_got, lambda: pass_raw(p, parity).wait_send(), nothing)
        return carry

    lax.fori_loop(0, pieces, drain, 0)

    def drain_out(e, carry):
        @pl.when(slab > 0)
        def _():
            ret_copy(e).wait_send()
            les_copy(e).wait_send()

        for part in range(2):
            ret_store(e, part).wait()
            les_store(e, part).wait()
        return carry

    lax.fori_loop(0, ne, drain_out, 0)


def body(
    energies, onsite, hamiltonian, hopping, contact, previous, neighbours, mode_index, mode_strength
):
    slabs, points = lax.axis_size("slab"), lax.axis_size("kt")
    ne, b = energies.shape[0], onsite.shape[-1]
    pieces = 2 * ne
    block = (pieces, 2, b, b)
    cat, square = (b, 2 * b), (2 * b, 2 * b)
    smem = pl.BlockSpec(memory_space=pltpu.SMEM)
    vmem = pl.BlockSpec(memory_space=pltpu.VMEM)
    anywhere = pl.BlockSpec(memory_space=pl.ANY)
    dma = pltpu.SemaphoreType.DMA
    table, plan = pl.pallas_call(
        functools.partial(agree, points, b),
        out_shape=(jax.ShapeDtypeStruct((16, b), F32), jax.ShapeDtypeStruct((1, 1), F32)),
        in_specs=[smem] * 4,
        out_specs=(vmem, smem),
        scratch_shapes=[
            pltpu.VMEM((8, 128), F32),
            pltpu.VMEM((points, 8, 128), F32),
            dma((points,)),
            dma((points,)),
        ],
        compiler_params=pltpu.CompilerParams(collective_id=0, has_side_effects=True),
        name="agree",
    )(energies, neighbours, mode_index, mode_strength)
    out = jax.ShapeDtypeStruct((ne, 2, b, b), BF16)

    def sweep(plan, *operands):
        halve = plan != WHOLE
        return pl.pallas_call(
            functools.partial(kernel, plan, slabs, points, ne, b),
            out_shape=(out, out),
            in_specs=[smem] + [vmem] * 5 + [anywhere],
            out_specs=(anywhere, anywhere),
            scratch_shapes=[
                pltpu.VMEM(block, BF16),
                pltpu.VMEM(block, BF16),
                pltpu.VMEM(block, BF16),
                pltpu.VMEM(block, BF16),
                pltpu.VMEM((pieces, b, b) if halve else (1, 16, 128), BF16),
                pltpu.VMEM((ne,) + cat, BF16),
                pltpu.VMEM((ne,) + cat, BF16),
                pltpu.VMEM(square, BF16),
                pltpu.VMEM((ne, 2) + square, BF16),
                pltpu.VMEM((ne,) + cat, BF16),
                pltpu.VMEM(square, BF16),
                pltpu.VMEM(square, BF16),
                pltpu.VMEM(cat, BF16),
                pltpu.VMEM(cat, BF16),
                pltpu.VMEM(cat, F32),
                pltpu.VMEM(cat, F32),
            ]
            + [dma((pieces,))] * 11
            + [dma((pieces, 2))]
            + [dma((AHEAD * 2 * (b // 128),))] * 4,
            compiler_params=pltpu.CompilerParams(
                collective_id=1 + plan,
                has_side_effects=True,
                vmem_limit_bytes=50 * 1024 * 1024,
            ),
            name=("sweep_whole", "sweep_seam", "sweep_down", "sweep_up")[plan],
        )(*operands)

    retarded, lesser = lax.switch(
        plan[0, 0].astype(jnp.int32),
        [functools.partial(sweep, which) for which in (WHOLE, SEAM, DOWN, UP)],
        energies, table, onsite[0], hamiltonian[0, 0], hopping[0, 0], contact[0],
        previous.reshape((ne, 2, 2, b, b)),
    )
    whole = (1, ne, 1, 2, b, b)
    return retarded.reshape(whole), lesser.reshape(whole)


def solution(mesh):
    in_specs = (
        P(),
        P("kt", "slab", None),
        P("kt", "slab", None, None, None),
        P("kt", "slab", None, None, None),
        P("kt", None, None, None),
        P("kt", None, "slab", None, None, None, None),
        P("kt", None),
        P("kt", None),
        P(),
    )
    out_specs = (P("kt", None, "slab", None, None, None), P("kt", None, "slab", None, None, None))
    return jax.shard_map(body, mesh=mesh, in_specs=in_specs, out_specs=out_specs, check_vma=False)
```

```python
import functools

import jax
import jax.numpy as jnp
from jax import lax
from jax.experimental import pallas as pl
from jax.experimental.pallas import tpu as pltpu
from jax.sharding import PartitionSpec as P

broaden = 0.05
fermi_level = 0.0
thermal = 0.1

MESH = pl.DeviceIdType.MESH
LEAD = 4
AHEAD = 2
F32 = jnp.float32
BF16 = jnp.bfloat16


def dot(a, b):
    return jnp.dot(a, b, preferred_element_type=F32)


def dot_nt(a, b):
    return lax.dot_general(a, b, (((1,), (1,)), ((), ())), preferred_element_type=F32)


def agree(
    points, b,
    energies, neighbours, mode_index, mode_strength,
    table, plan,
    mine, every, send, recv,
):
    k = lax.axis_index("kt")
    even = lax.rem(k, 2) == 0
    barrier = pltpu.get_barrier_semaphore()

    def peer(by):
        return {"kt": lax.rem(k + by, points)}

    def greet(by, carry):
        pl.semaphore_signal(barrier, inc=1, device_id=peer(by), device_id_type=MESH)
        return carry

    lax.fori_loop(1, points, greet, 0)
    pl.semaphore_wait(barrier, points - 1)
    left = jnp.where(neighbours[0, 0] == lax.rem(k - 1 + points, points), 1.0, 0.0)
    right = jnp.where(neighbours[0, 1] == lax.rem(k + 1, points), 1.0, 0.0)
    row = lax.broadcasted_iota(jnp.int32, (8, 128), 0)
    mine[...] = jnp.where(row == 0, left, right)
    every[k] = mine[...]

    def tell(by):
        return pltpu.make_async_remote_copy(
            mine, every.at[k], send.at[by], recv.at[k], device_id=peer(by), device_id_type=MESH
        )

    def hear(by):
        j = lax.rem(k + by, points)
        return pltpu.make_async_remote_copy(
            mine, every.at[j], send.at[by], recv.at[j], device_id=peer(by), device_id_type=MESH
        )

    def start(by, carry):
        tell(by).start()
        return carry

    def finish(by, carry):
        tell(by).wait_send()
        hear(by).wait_recv()
        return carry

    lax.fori_loop(1, points, start, 0)
    lax.fori_loop(1, points, finish, 0)

    def near(j):
        j = lax.rem(j + points, points)
        return every[j, 0:1, :], every[j, 1:2, :]

    left_2, right_2 = near(k + 2), near(k - 2)
    left_1, right_1 = near(k + 1), near(k - 1)
    chosen = jnp.where(even, left_2[0], right_2[1])
    wrapped = jnp.where(even, right_1[1], left_1[0])
    strength_left = mode_strength[mode_index[0, 0]]
    strength_right = mode_strength[mode_index[0, 1]]
    weight_sel = jnp.where(even, strength_left, strength_right)
    weight_other = jnp.where(even, strength_right, strength_left)
    other_near = jnp.where(even, right, left)
    full = jnp.zeros((1, 128), F32)
    rows = [
        chosen,
        wrapped,
        full + weight_sel,
        full + weight_other * other_near,
        full + weight_other * (1.0 - other_near),
    ]
    for e in range(energies.shape[0]):
        rows.append(1.0 / (1.0 + jnp.exp((full + energies[e] - fermi_level) / thermal)))
    for i, value in enumerate(rows):
        for start_at in range(0, b, 128):
            table[i : i + 1, start_at : start_at + 128] = value

    def pair_far(m):
        first, second = near(2 * m), near(2 * m + 1)
        return (1.0 - first[0]) * (1.0 - second[0]), (1.0 - first[1]) * (1.0 - second[1])

    def gather(m, found):
        up, down = pair_far(m)
        return jnp.maximum(found[0], up), jnp.maximum(found[1], down)

    up, down = lax.fori_loop(0, points // 2, gather, (full, full))
    seam = jnp.maximum(pair_far(0)[0], pair_far(points // 2 - 1)[1])
    plan[0, 0] = jnp.max(1.0 - seam + seam * (2.0 * (1.0 - down) + down * 3.0 * (1.0 - up)))


WHOLE, SEAM, DOWN, UP = range(4)


def kernel(
    plan, slabs, points, ne, b,
    energies, table, onsite, ham, hop, contact, prev,
    ret_out, les_out,
    own, mate, zsel, zraw, stage, bx, bl, chat, pair, les, wide, fhat, mv, sysb, acc, first,
    own_sem, y_send, y_recv, s_send, s_recv, r_send, r_recv, f_send, f_recv, b_send, b_recv, o_sem,
    u_send, u_recv, v_send, v_recv,
):
    slab = lax.axis_index("slab")
    k = lax.axis_index("kt")
    pieces = 2 * ne
    step = 2 - 4 * lax.rem(k, 2)
    parity = lax.rem(k, 2)
    mate_k = k + 1 - 2 * lax.rem(k, 2)
    sel_k = lax.rem(k + step + points, points)
    raw_k = lax.rem(k - step + points, points)
    halve = plan != WHOLE
    even = parity == 0
    odd = parity == 1
    if plan == SEAM:
        raw_cut = jnp.logical_or(k == 0, k == points - 1)
        sel_cut = jnp.logical_or(k == 1, k == points - 2)
        raw_got, sel_got = sel_cut, raw_cut
    elif plan == DOWN:
        raw_cut, sel_cut, raw_got, sel_got = even, odd, even, odd
    else:
        raw_cut, sel_cut, raw_got, sel_got = odd, even, odd, even
    last = slabs - 1
    bands = [(n, min(256, 2 * b - n)) for n in range(0, 2 * b, 256)]
    rows_per = 48

    barrier = pltpu.get_barrier_semaphore()
    for other in (mate_k, sel_k, raw_k):
        pl.semaphore_signal(barrier, inc=1, device_id={"kt": other}, device_id_type=MESH)
    for by in (1, slabs - 1):
        pl.semaphore_signal(
            barrier, inc=1, device_id={"slab": lax.rem(slab + by, slabs)}, device_id_type=MESH
        )
    pl.semaphore_wait(barrier, 5)

    def source(p):
        return prev.at[lax.rem(p, ne), p // ne]

    def y_copy(p):
        return pltpu.make_async_remote_copy(
            source(p), mate.at[p], y_send.at[p], y_recv.at[p],
            device_id={"kt": mate_k}, device_id_type=MESH,
        )

    def raw_copy(p):
        return pltpu.make_async_remote_copy(
            source(p), zraw.at[p], r_send.at[p], r_recv.at[p],
            device_id={"kt": raw_k}, device_id_type=MESH,
        )

    def sel_copy(p):
        return pltpu.make_async_remote_copy(
            own.at[p], zsel.at[p], s_send.at[p], s_recv.at[p],
            device_id={"kt": sel_k}, device_id_type=MESH,
        )

    per = 2 * (b // 128)
    units = AHEAD * per

    def unit(i, part):
        j = lax.rem(i, per)
        part = jnp.where(j < per // 2, part, 1 - part)
        return part, pl.ds(pl.multiple_of(lax.rem(j, per // 2) * 128, 128), 128)

    def y_unit(i, part):
        return pltpu.make_async_remote_copy(
            source(i // per).at[unit(i, part)], mate.at[i // per].at[unit(i, part)],
            u_send.at[i], u_recv.at[i], device_id={"kt": mate_k}, device_id_type=MESH,
        )

    def sel_unit(i):
        return pltpu.make_async_remote_copy(
            own.at[i // per].at[unit(i, parity)], zsel.at[i // per].at[unit(i, parity)],
            v_send.at[i], v_recv.at[i], device_id={"kt": sel_k}, device_id_type=MESH,
        )

    def wait_sel(p):
        @pl.when(p < AHEAD)
        def _():
            def one(j, carry):
                sel_unit(p * per + j).wait_recv()
                return carry

            lax.fori_loop(0, per, one, 0)

        @pl.when(p >= AHEAD)
        def _():
            sel_copy(p).wait_recv()

    def own_copy(p):
        return pltpu.make_async_copy(source(p), own.at[p], own_sem.at[p])

    def raw_half(p):
        return pltpu.make_async_remote_copy(
            stage.at[p], zraw.at[p, parity], r_send.at[p], r_recv.at[p],
            device_id={"kt": raw_k}, device_id_type=MESH,
        )

    def sel_half(p):
        return pltpu.make_async_remote_copy(
            stage.at[p], zsel.at[p, parity], s_send.at[p], s_recv.at[p],
            device_id={"kt": sel_k}, device_id_type=MESH,
        )

    def pass_sel(p, part):
        return pltpu.make_async_remote_copy(
            zsel.at[p, part], zraw.at[p, part], f_send.at[p], f_recv.at[p],
            device_id={"kt": mate_k}, device_id_type=MESH,
        )

    def pass_raw(p, part):
        return pltpu.make_async_remote_copy(
            zraw.at[p, part], zsel.at[p, part], f_send.at[p], f_recv.at[p],
            device_id={"kt": mate_k}, device_id_type=MESH,
        )

    def either(seam, half, whole):
        if not halve:
            whole()
            return
        pl.when(seam)(half)
        pl.when(jnp.logical_not(seam))(whole)

    def nothing():
        return None

    def pass_on(p):
        if not halve:
            return

        @pl.when(sel_got)
        def _():
            sel_half(p).wait_recv()
            pass_sel(p, parity).start()

        @pl.when(raw_got)
        def _():
            raw_half(p).wait_recv()
            pass_raw(p, parity).start()

    def arrived(p):
        either(sel_got, lambda: pass_raw(p, 1 - parity).wait_recv(), lambda: wait_sel(p))
        either(raw_got, lambda: pass_sel(p, 1 - parity).wait_recv(), lambda: raw_copy(p).wait_recv())

    def ret_copy(e):
        return pltpu.make_async_remote_copy(
            pair.at[e, 0, pl.ds(0, b)], bx.at[e], b_send.at[e], b_recv.at[e],
            device_id={"slab": jnp.maximum(slab - 1, 0)}, device_id_type=MESH,
        )

    def les_copy(e):
        return pltpu.make_async_remote_copy(
            les.at[e], bl.at[e], b_send.at[ne + e], b_recv.at[ne + e],
            device_id={"slab": jnp.maximum(slab - 1, 0)}, device_id_type=MESH,
        )

    def ret_store(e, part):
        return pltpu.make_async_copy(
            pair.at[e, 0, pl.ds(0, b), pl.ds(part * b, b)], ret_out.at[e, part], o_sem.at[e, part]
        )

    def les_store(e, part):
        return pltpu.make_async_copy(
            les.at[e, :, pl.ds(part * b, b)], les_out.at[e, part], o_sem.at[ne + e, part]
        )

    def begin(p):
        y_copy(p).start()
        own_copy(p).start()

    def begin_raw(p):
        either(raw_cut, nothing, lambda: raw_copy(p).start())

    def every_unit(do):
        def one(i, carry):
            do(i)
            return carry

        lax.fori_loop(0, units, one, 0)

    every_unit(lambda i: y_unit(i, 1 - parity).start())
    for p in range(AHEAD):
        own_copy(p).start()
    begin_raw(0)
    either(sel_cut, nothing, lambda: begin_raw(1))

    def expand(ref):
        ref[b:, 0:b] = -ref[0:b, b:]
        ref[b:, b:] = ref[0:b, 0:b]

    chat[0:b, 0:b] = hop[0]
    chat[0:b, b:] = hop[1]
    expand(chat)

    @pl.when(slab == last)
    def _():
        for part in range(2):
            value = contact[part].astype(F32)
            flipped = value.T
            skew = value - flipped if part == 0 else value + flipped
            acc[:, part * b : (part + 1) * b] = skew
            for e in range(ne):
                bx[e, :, part * b : (part + 1) * b] = contact[part]
        for e in range(ne):
            for part in range(2):
                columns = slice(part * b, (part + 1) * b)
                bl[e, :, columns] = (-table[5 + e : 6 + e, :] * acc[:, columns]).astype(BF16)

    def phonon(p, part, rows):
        return (
            table[2:3, :] * zsel[p, part, rows].astype(F32)
            + table[3:4, :] * mate[p, part, rows].astype(F32)
            + table[4:5, :] * zraw[p, part, rows].astype(F32)
        )

    def over_rows(do, unroll=False):
        def one(i, carry):
            do(pl.ds(pl.multiple_of(i * rows_per, rows_per), rows_per))
            return carry

        lax.fori_loop(0, b // rows_per, one, 0, unroll=unroll)

    def mixed(chosen, p, part, rows):
        return (
            chosen * mate[p, part, rows].astype(F32) + (1.0 - chosen) * own[p, part, rows].astype(F32)
        ).astype(BF16)

    def half_choice():
        return jnp.where(raw_cut, 1.0 - table[1:2, :], table[0:1, :])

    def start_half(p):
        pl.when(raw_cut)(lambda: raw_half(p).start())
        pl.when(sel_cut)(lambda: sel_half(p).start())

    def meet_unit(i, carry):
        p, j = i // per, lax.rem(i, per)

        @pl.when(j == 0)
        def _():
            own_copy(p).wait()

        y_unit(i, parity).wait_recv()
        part, rows = unit(i, parity)
        if halve:

            @pl.when(jnp.logical_and(jnp.logical_or(raw_cut, sel_cut), j < per // 2))
            def _():
                stage[p, rows] = mixed(half_choice(), p, part, rows)
                pl.when(j == per // 2 - 1)(lambda: start_half(p))

        def start_sel():
            own[p, part, rows] = mixed(table[0:1, :], p, part, rows)
            sel_unit(i).start()

        either(sel_cut, nothing, start_sel)

        @pl.when(j == per - 1)
        def _():
            begin(p + AHEAD)
            if halve:
                pl.when(jnp.logical_and(sel_cut, p + 1 < AHEAD))(lambda: begin_raw(p + 1))

        return carry

    def meet(p):
        y_copy(p).wait_recv()
        own_copy(p).wait()

        if halve:

            @pl.when(jnp.logical_or(raw_cut, sel_cut))
            def _():
                chosen = half_choice()

                def pick(rows):
                    stage[p, rows] = mixed(chosen, p, parity, rows)

                over_rows(pick)
                start_half(p)

        either(sel_cut, lambda: begin_raw(p), nothing)

        @pl.when(p + 1 < pieces)
        def _():
            either(sel_cut, nothing, lambda: begin_raw(p + 1))

        @pl.when(p + AHEAD < pieces)
        def _():
            begin(p + AHEAD)

    def prep(p):
        def pick(rows):
            for part in range(2):
                own[p, part, rows] = mixed(table[0:1, :], p, part, rows)

        def start_sel():
            over_rows(pick)
            sel_copy(p).start()

        either(sel_cut, nothing, start_sel)

    def self_energy(boundary):
        wide[0:b, :] = boundary[...]
        expand(wide)
        for n, w in bands:
            mv[:, n : n + w] = dot(chat[0:b, :], wide[:, n : n + w]).astype(BF16)
        for n, w in bands:
            acc[:, n : n + w] = dot_nt(mv[...], chat[n : n + w, :])

    def ret_stage(e):
        @pl.when(slab < last)
        def _():
            ret_copy(e).wait_recv()

        self_energy(bx.at[e])
        arrived(e)
        energy = energies[e]

        def make_system(rows):
            at = lax.broadcasted_iota(jnp.int32, (rows_per, b), 0) + rows.start
            eye = at == lax.broadcasted_iota(jnp.int32, (rows_per, b), 1)
            real = jnp.where(eye, energy - onsite[...], 0.0)
            imag = jnp.where(eye, broaden, 0.0)
            for part, diagonal in ((0, real), (1, imag)):
                columns = slice(part * b, (part + 1) * b)
                value = (
                    diagonal - ham[part, rows].astype(F32) - acc[rows, columns] - phonon(e, part, rows)
                )
                acc[rows, columns] = value
                sysb[rows, columns] = value.astype(BF16)

        over_rows(make_system)
        eye = lax.broadcasted_iota(jnp.int32, (128, 128), 0) == lax.broadcasted_iota(
            jnp.int32, (128, 128), 1
        )
        across, along = [], []
        for i in range(b // 128):
            rows = slice(i * 128, (i + 1) * 128)
            real = jnp.where(eye, acc[rows, i * 128 : (i + 1) * 128], 0.0)
            imag = jnp.where(eye, acc[rows, b + i * 128 : b + (i + 1) * 128], 0.0)
            for axis, found in ((0, across), (1, along)):
                re = jnp.sum(real, axis=axis, keepdims=True)
                im = jnp.sum(imag, axis=axis, keepdims=True)
                modulus = re * re + im * im
                found.append((re / modulus, -im / modulus))
        row_re = jnp.concatenate([found[0] for found in across], axis=1)
        row_im = jnp.concatenate([found[1] for found in across], axis=1)
        for i in range(b // 128):
            col_re, col_im = along[i]
            for half in range(2):
                start = i * 128 + half * 64
                rows = slice(start, start + 64)
                cre = col_re[half * 64 : half * 64 + 64]
                cim = col_im[half * 64 : half * 64 + 64]
                re, im = acc[rows, 0:b], acc[rows, b:]
                scaled_re = cre * re - cim * im
                scaled_im = cre * im + cim * re
                on = (
                    lax.broadcasted_iota(jnp.int32, (64, b), 0) + start
                    == lax.broadcasted_iota(jnp.int32, (64, b), 1)
                )
                first_re = jnp.where(on, 2.0 * row_re, 0.0) - (scaled_re * row_re - scaled_im * row_im)
                first_im = jnp.where(on, 2.0 * row_im, 0.0) - (scaled_re * row_im + scaled_im * row_re)
                first[rows, 0:b] = first_re
                first[rows, b:] = first_im
                fhat[rows, 0:b] = first_re.astype(BF16)
                fhat[rows, b:] = first_im.astype(BF16)
        expand(fhat)
        for n, w in bands:
            wide[0:b, n : n + w] = dot(sysb[...], fhat[:, n : n + w]).astype(BF16)
        expand(wide)
        for n, w in bands:
            pair[e, 0, 0:b, n : n + w] = (
                2.0 * first[:, n : n + w] - dot(fhat[0:b, :], wide[:, n : n + w])
            ).astype(BF16)

        @pl.when(slab > 0)
        def _():
            ret_copy(e).start()

        ret_store(e, 0).start()
        ret_store(e, 1).start()
        expand(pair.at[e, 0])
        for n, w in bands:
            pair[e, 1, 0:b, n : n + w] = dot(pair[e, 0, 0:b, :], chat[:, n : n + w]).astype(BF16)
        expand(pair.at[e, 1])

    def les_stage(e):
        p = ne + e
        acc[...] = jnp.zeros_like(acc)

        def term(i, carry):
            which = jnp.where(slab == last, 1 - i, i)

            @pl.when(which == 0)
            def _():
                arrived(p)

                def make_source(rows):
                    real, imag = (phonon(p, part, rows).astype(BF16) for part in range(2))
                    below = pl.ds(b + rows.start, rows.size)
                    wide[rows, 0:b] = real
                    wide[rows, b:] = imag
                    wide[below, 0:b] = -imag
                    wide[below, b:] = real

                over_rows(make_source, True)

            @pl.when(which == 1)
            def _():
                pl.when(slab < last)(lambda: les_copy(e).wait_recv())
                wide[0:b, :] = bl[e]
                wide[b:, 0:b] = -bl[e, :, b:]
                wide[b:, b:] = bl[e, :, 0:b]

            for n, w in bands:
                mv[:, n : n + w] = dot(pair[e, which, 0:b, :], wide[:, n : n + w]).astype(BF16)
            for n, w in bands:
                total = acc[:, n : n + w] + dot_nt(mv[...], pair[e, which, n : n + w, :])
                acc[:, n : n + w] = total
                les[e, :, n : n + w] = total.astype(BF16)
            return carry

        lax.fori_loop(0, 2, term, 0)

        @pl.when(slab > 0)
        def _():
            les_copy(e).start()

        les_store(e, 0).start()
        les_store(e, 1).start()

    def turn(t, carry):
        @pl.when(jnp.logical_and(t >= AHEAD, t < pieces))
        def _():
            prep(t)

        @pl.when(jnp.logical_and(t + 1 >= AHEAD, t + 1 < pieces))
        def _():
            meet(t + 1)

        c = t - LEAD

        @pl.when(jnp.logical_and(c + 1 >= 0, c + 1 < pieces))
        def _():
            pass_on(c + 1)

        @pl.when(jnp.logical_and(c >= 0, c < ne))
        def _():
            ret_stage(c)

        @pl.when(c >= ne)
        def _():
            les_stage(c - ne)

        return carry

    lax.fori_loop(0, units, meet_unit, 0)
    either(sel_cut, nothing, lambda: begin_raw(AHEAD))
    lax.fori_loop(0, pieces + LEAD, turn, 0)

    every_unit(lambda i: y_unit(i, 1 - parity).wait_send())
    either(sel_cut, nothing, lambda: every_unit(lambda i: sel_unit(i).wait_send()))

    def drain(p, carry):
        @pl.when(p >= AHEAD)
        def _():
            y_copy(p).wait_send()
            either(sel_cut, nothing, lambda: sel_copy(p).wait_send())

        either(raw_cut, lambda: raw_half(p).wait_send(), lambda: raw_copy(p).wait_send())
        either(sel_cut, lambda: sel_half(p).wait_send(), nothing)
        either(sel_got, lambda: pass_sel(p, parity).wait_send(), nothing)
        either(raw_got, lambda: pass_raw(p, parity).wait_send(), nothing)
        return carry

    lax.fori_loop(0, pieces, drain, 0)

    def drain_out(e, carry):
        @pl.when(slab > 0)
        def _():
            ret_copy(e).wait_send()
            les_copy(e).wait_send()

        for part in range(2):
            ret_store(e, part).wait()
            les_store(e, part).wait()
        return carry

    lax.fori_loop(0, ne, drain_out, 0)


def body(
    energies, onsite, hamiltonian, hopping, contact, previous, neighbours, mode_index, mode_strength
):
    slabs, points = lax.axis_size("slab"), lax.axis_size("kt")
    ne, b = energies.shape[0], onsite.shape[-1]
    pieces = 2 * ne
    block = (pieces, 2, b, b)
    cat, square = (b, 2 * b), (2 * b, 2 * b)
    smem = pl.BlockSpec(memory_space=pltpu.SMEM)
    vmem = pl.BlockSpec(memory_space=pltpu.VMEM)
    anywhere = pl.BlockSpec(memory_space=pl.ANY)
    dma = pltpu.SemaphoreType.DMA
    table, plan = pl.pallas_call(
        functools.partial(agree, points, b),
        out_shape=(jax.ShapeDtypeStruct((16, b), F32), jax.ShapeDtypeStruct((1, 1), F32)),
        in_specs=[smem] * 4,
        out_specs=(vmem, smem),
        scratch_shapes=[
            pltpu.VMEM((8, 128), F32),
            pltpu.VMEM((points, 8, 128), F32),
            dma((points,)),
            dma((points,)),
        ],
        compiler_params=pltpu.CompilerParams(collective_id=0, has_side_effects=True),
        name="agree",
    )(energies, neighbours, mode_index, mode_strength)
    out = jax.ShapeDtypeStruct((ne, 2, b, b), BF16)

    def sweep(plan, *operands):
        halve = plan != WHOLE
        return pl.pallas_call(
            functools.partial(kernel, plan, slabs, points, ne, b),
            out_shape=(out, out),
            in_specs=[smem] + [vmem] * 5 + [anywhere],
            out_specs=(anywhere, anywhere),
            scratch_shapes=[
                pltpu.VMEM(block, BF16),
                pltpu.VMEM(block, BF16),
                pltpu.VMEM(block, BF16),
                pltpu.VMEM(block, BF16),
                pltpu.VMEM((pieces, b, b) if halve else (1, 16, 128), BF16),
                pltpu.VMEM((ne,) + cat, BF16),
                pltpu.VMEM((ne,) + cat, BF16),
                pltpu.VMEM(square, BF16),
                pltpu.VMEM((ne, 2) + square, BF16),
                pltpu.VMEM((ne,) + cat, BF16),
                pltpu.VMEM(square, BF16),
                pltpu.VMEM(square, BF16),
                pltpu.VMEM(cat, BF16),
                pltpu.VMEM(cat, BF16),
                pltpu.VMEM(cat, F32),
                pltpu.VMEM(cat, F32),
            ]
            + [dma((pieces,))] * 11
            + [dma((pieces, 2))]
            + [dma((AHEAD * 2 * (b // 128),))] * 4,
            compiler_params=pltpu.CompilerParams(
                collective_id=1 + plan,
                has_side_effects=True,
                vmem_limit_bytes=50 * 1024 * 1024,
            ),
            name=("sweep_whole", "sweep_seam", "sweep_down", "sweep_up")[plan],
        )(*operands)

    retarded, lesser = lax.switch(
        plan[0, 0].astype(jnp.int32),
        [functools.partial(sweep, which) for which in (WHOLE, SEAM, DOWN, UP)],
        energies, table, onsite[0], hamiltonian[0, 0], hopping[0, 0], contact[0],
        previous.reshape((ne, 2, 2, b, b)),
    )
    whole = (1, ne, 1, 2, b, b)
    return retarded.reshape(whole), lesser.reshape(whole)


def solution(mesh):
    in_specs = (
        P(),
        P("kt", "slab", None),
        P("kt", "slab", None, None, None),
        P("kt", "slab", None, None, None),
        P("kt", None, None, None),
        P("kt", None, "slab", None, None, None, None),
        P("kt", None),
        P("kt", None),
        P(),
    )
    out_specs = (P("kt", None, "slab", None, None, None), P("kt", None, "slab", None, None, None))
    return jax.shard_map(body, mesh=mesh, in_specs=in_specs, out_specs=out_specs, check_vma=False)
```
